512 devices in a mesh: dp: 8 (over y), tensor: 4 (over z_hi, core), expert: 16 (over x, z_lo).
Axes of the slice: x: 4, y: 8, z: 8 (z_hi: 2, z_lo: 4; z = z_hi * 4 + z_lo), core: 2. Of those that a mesh axis runs over, the one named last changes fastest.
Arguments:
- tokens: bfloat16 [4096, 2048], P('dp', 'tensor'), may hold values from -6 to 6
- grad_out: bfloat16 [4096, 2048], P('dp', 'tensor'), may hold values from -6 to 6
- routes: int32 [4096, 8], P('dp'), may hold values from 0 to 127, all different within a row; in each aligned block of 512 rows (0 to 511, 512 to 1023, ...) at most 48 rows name the same one
- gates: float32 [4096, 8], P('dp'), may hold values from 0.03 to 0.3
- gate_weight: bfloat16 [64, 1536, 2048], P(('expert', 'tensor'), 'dp'), may hold values from -0.125 to 0.125
- up_weight: bfloat16 [64, 1536, 2048], P(('expert', 'tensor'), 'dp'), may hold values from -0.125 to 0.125
- down_weight: bfloat16 [64, 1536, 2048], P(('expert', 'tensor'), 'dp'), may hold values from -0.15625 to 0.15625
Outputs:
- mixed: bfloat16 [4096, 2048], P('dp', 'tensor')
- grad_tokens: bfloat16 [4096, 2048], P('dp', 'tensor')
- grad_gates: float32 [4096, 8], P('dp')
The draws below stay inside these ranges and needn't reach their ends.
Inputs may be any that keep to these rules, and one draw needn't show every extreme that they name: `routes`: each row names 8 different experts. Among the 512 rows of one block no expert is named more than 48 times, a bound that some block reaches.
All inputs are finite; a program needn't handle non-finite values.
Results may differ from the reference program's by a relative error of at most 0.017.
Values may be sent and summed in bfloat16 or wider, within the bound.
A program may use at most 64 MiB of HBM per device.

```python
import math
import jax
import jax.numpy as jnp
import numpy as np
from jax import lax

D = 2048
FF = 1536
ALL_EXPERTS = 128
TOPK = 8
TOK_DEV = 512
CAP = 48
EXPERTS = 64
TOKENS = 4096
N_DP = 8
N_TENSOR = 4
N_EXPERT = 16


def block_scale(own_key, shape, shards, smallest, high):
    level = 1.0
    for position, shards_of in shards:
        steps = jax.random.uniform(jax.random.fold_in(jax.random.fold_in(own_key, 6), position), (shards_of,), jnp.float32, smallest / len(shards), high / len(shards))
        level = level * jnp.repeat(jnp.exp(steps), shape[position] // shards_of).reshape((-1,) + (1,) * (len(shape) - 1 - position))
    return level


def deal_out(stream_key, own, number, rows, amount, top, limit, lean):
    order = jax.random.permutation(stream_key, amount)
    crowded, ordinary = portions_of(amount, rows * top, limit, lean, True), portions_of(amount, rows * top, limit, lean, False)
    places = jnp.arange(amount)

    def named(lengths, offset_by):
        used = int((lengths > 0).sum())
        fixed = max(1, used // 4)
        moved = fixed + (places - fixed + offset_by * (used - fixed)) % max(1, amount - fixed)
        return jnp.zeros((amount,), jnp.int32).at[order[jnp.where(places < fixed, places, moved)]].set(jnp.asarray(lengths, jnp.int32))

    lengths = jnp.where(number % 4 == 0, named(crowded, number // 4), named(ordinary, number - number // 4 - 1))
    mixed = jax.random.permutation(jax.random.fold_in(own, 3), amount)
    donor, taker = mixed[0:amount // 2 * 2:2], mixed[1:amount // 2 * 2:2]
    slack = jnp.minimum(lengths[donor] - 1, limit - lengths[taker]) // 2
    slack = jnp.where((donor == order[0]) | (taker == order[0]) | (lengths[taker] == 0), 0, jnp.maximum(slack, 0))
    moved = jax.random.randint(jax.random.fold_in(own, 4), (amount // 2,), 0, 1 << 20) % (slack + 1)
    lengths = lengths.at[donor].add(-moved).at[taker].add(moved)
    labels = jnp.searchsorted(jnp.cumsum(lengths), jnp.arange(rows * top), side="right").astype(jnp.int32)
    listing = labels.reshape(top, rows).T
    listing = listing[jax.random.permutation(jax.random.fold_in(own, 1), rows)]
    offset_by = jax.random.randint(jax.random.fold_in(own, 2), (rows, 1), 0, top)
    return jnp.take_along_axis(listing, (jnp.arange(top)[None, :] + offset_by) % top, axis=1)


def portions_of(count, total, bound, skew, full):
    weights = [(1 << 20) // math.isqrt(grade ** skew) + 1 for grade in range(1, count + 1)]
    largest = bound if full else min(bound, max(-(-total // count), total * weights[0] // sum(weights)))
    least = 1 if total - largest >= count - 1 else 0
    holding, surplus = [largest] + [least] * (count - 1), total - largest - least * (count - 1)
    while surplus > 0:
        candidates = [i for i in range(1, count) if holding[i] < largest] or [i for i in range(1, count) if holding[i] < bound]
        mass, remaining = sum([weights[i] for i in candidates]), surplus
        for i in candidates:
            addition = min(bound - holding[i], max(1, remaining * weights[i] // mass), surplus)
            holding[i] = holding[i] + addition
            surplus = surplus - addition
    return np.array(holding)


def gaussian(stream_key, shape, spread, bound, pieces=(), kind=jnp.bfloat16):
    gain = block_scale(stream_key, shape, pieces, -0.22, 0.18) if pieces else 1.0
    values = jax.random.normal(stream_key, shape, jnp.float32) * spread * gain
    return jnp.minimum(jnp.maximum(values, -bound), bound).astype(kind)


def setup_inputs(seed: int = 0) -> dict:
    keys = jax.random.split(jax.random.key(seed), 8)
    tokens = gaussian(keys[0], (TOKENS, D), 1.0, 6.0, ((0, 8), (1, 4)))
    grad_out = gaussian(keys[1], (TOKENS, D), 1.0, 6.0, ((0, 8), (1, 4)))
    routes_keys = jax.random.split(jax.random.fold_in(keys[2], 1), TOKENS // TOK_DEV)
    routes_turns = jax.random.permutation(jax.random.fold_in(keys[2], 3), TOKENS // TOK_DEV)
    routes = jax.vmap(lambda own, number: deal_out(jax.random.fold_in(keys[2], 2), own, number, TOK_DEV, ALL_EXPERTS, TOPK, CAP, 1))(routes_keys, routes_turns).reshape((TOKENS, TOPK))
    gates = jnp.clip(jnp.exp(math.log(0.3) - 2.3025852 * jax.random.uniform(keys[3], (TOKENS, TOPK), jnp.float32) ** block_scale(keys[3], (TOKENS, TOPK), ((0, 8),), -0.2, 0.2)), 0.03, 0.3)
    gate_weight = gaussian(keys[4], (EXPERTS, FF, D), D ** -0.5, 0.125, ((0, 64), (1, 8)))
    up_weight = gaussian(keys[5], (EXPERTS, FF, D), D ** -0.5, 0.125, ((0, 64), (1, 8)))
    down_weight = gaussian(keys[6], (EXPERTS, FF, D), FF ** -0.5, 0.15625, ((0, 64), (1, 8)))
    return dict(tokens=tokens, grad_out=grad_out, routes=routes, gates=gates, gate_weight=gate_weight, up_weight=up_weight, down_weight=down_weight)


def silu_parts(gate_pre):
    sigmoid_val = jax.nn.sigmoid(gate_pre)
    return gate_pre * sigmoid_val, sigmoid_val * (1.0 + gate_pre * (1.0 - sigmoid_val))


def slot_numbers(route_block):
    flat_ids = route_block.reshape(-1)
    onehot = (flat_ids[:, None] == jnp.arange(EXPERTS, dtype=jnp.int32)[None, :]).astype(jnp.int32)
    ranking = jnp.sum((jnp.cumsum(onehot, axis=0) - 1) * onehot, axis=1).astype(jnp.int32)
    slot_ids = jnp.where(flat_ids < EXPERTS, flat_ids * CAP + ranking, -1).astype(jnp.int32)
    return slot_ids.reshape(TOK_DEV, TOPK)


def selector(slot_ids, number):
    return slot_ids[None, :, :] == jnp.arange(number, dtype=jnp.int32)[:, None, None]


def rounded(values):
    return lax.optimization_barrier(values.astype(jnp.bfloat16)).astype(jnp.float32)


def reference(tokens, grad_out, routes, gates, gate_weight, up_weight, down_weight):
    hid_dev = FF // N_DP
    contract = (((1,), (1,)), ((), ()))
    slots_all = lax.map(slot_numbers, routes.reshape(N_DP, TOK_DEV, TOPK))

    def dispatch(operands):
        tok_block, grad_block, slot_block = operands
        picker = jnp.any(selector(slot_block, EXPERTS * CAP), axis=2).astype(jnp.bfloat16)
        sent_tok = jnp.dot(picker, tok_block, preferred_element_type=jnp.float32).astype(jnp.bfloat16)
        sent_grad = jnp.dot(picker, grad_block, preferred_element_type=jnp.float32).astype(jnp.bfloat16)
        return sent_tok, sent_grad

    sent_tok, sent_grad = lax.map(dispatch, (tokens.reshape(N_DP, TOK_DEV, D), grad_out.reshape(N_DP, TOK_DEV, D), slots_all))

    def to_experts(values):
        return values.reshape(N_DP, EXPERTS, CAP, D).transpose(1, 0, 2, 3).reshape(EXPERTS, N_DP * CAP, D)

    def expert(operands):
        rows_in, rows_grad, w_gate, w_up, w_down = operands
        gate_pre = lax.dot_general(rows_in, w_gate, contract, preferred_element_type=jnp.float32)
        up_pre = lax.dot_general(rows_in, w_up, contract, preferred_element_type=jnp.float32)
        activated, slope_val = silu_parts(gate_pre)
        hidden = (activated * up_pre).astype(jnp.bfloat16)
        hid_blocks = hidden.astype(jnp.float32).reshape(-1, N_DP, hid_dev)
        down_blocks = w_down.astype(jnp.float32).reshape(N_DP, hid_dev, D)
        partials = jnp.einsum("rjf,jfd->jrd", hid_blocks, down_blocks, precision=lax.Precision.HIGHEST)
        expert_out = jnp.sum(rounded(partials), axis=0).astype(jnp.bfloat16)
        grad_hid = lax.dot_general(rows_grad, w_down, contract, preferred_element_type=jnp.float32)
        grad_gate = (grad_hid * (up_pre * slope_val)).astype(jnp.bfloat16)
        grad_up = (grad_hid * activated).astype(jnp.bfloat16)
        gate_blocks = w_gate.astype(jnp.float32).reshape(N_DP, hid_dev, D)
        up_blocks = w_up.astype(jnp.float32).reshape(N_DP, hid_dev, D)
        back_parts = jnp.einsum("rjf,jfd->jrd", grad_gate.astype(jnp.float32).reshape(-1, N_DP, hid_dev), gate_blocks, precision=lax.Precision.HIGHEST)
        back_parts = back_parts + jnp.einsum("rjf,jfd->jrd", grad_up.astype(jnp.float32).reshape(-1, N_DP, hid_dev), up_blocks, precision=lax.Precision.HIGHEST)
        expert_back = jnp.sum(rounded(back_parts), axis=0).astype(jnp.bfloat16)
        slot_grads = jnp.sum(expert_out.astype(jnp.float32) * rows_grad.astype(jnp.float32), axis=1)
        return expert_out, expert_back, slot_grads

    outs, backs, slot_grads = lax.map(expert, (to_experts(sent_tok), to_experts(sent_grad), gate_weight, up_weight, down_weight))

    def to_blocks(values):
        return values.reshape(EXPERTS, N_DP, CAP, D).transpose(1, 0, 2, 3).reshape(N_DP, EXPERTS * CAP, D)

    grad_blocks = slot_grads.reshape(EXPERTS, N_DP, CAP).transpose(1, 0, 2).reshape(N_DP, EXPERTS * CAP)

    def combine(operands):
        slot_block, gate_block, out_block, back_block, grad_block = operands
        choose = selector(slot_block, EXPERTS * CAP).astype(jnp.float32)
        weighted = jnp.einsum("stk,tk->ts", choose, gate_block, precision=lax.Precision.HIGHEST).astype(jnp.bfloat16)
        grouped = weighted.astype(jnp.float32).reshape(TOK_DEV, N_EXPERT, N_TENSOR * CAP)

        def group_sum(slot_rows):
            rows_grouped = slot_rows.astype(jnp.float32).reshape(N_EXPERT, N_TENSOR * CAP, D)
            parts = jnp.einsum("tgs,gsd->gtd", grouped, rows_grouped, precision=lax.Precision.HIGHEST)
            return jnp.sum(rounded(parts), axis=0).astype(jnp.bfloat16)

        mixed = group_sum(out_block)
        grad_tokens = group_sum(back_block)
        grad_gates = jnp.einsum("stk,s->tk", choose, grad_block, precision=lax.Precision.HIGHEST)
        return mixed, grad_tokens, grad_gates

    mixed, grad_tokens, grad_gates = lax.map(combine, (slots_all, gates.reshape(N_DP, TOK_DEV, TOPK), to_blocks(outs), to_blocks(backs), grad_blocks))
    return mixed.reshape(TOKENS, D), grad_tokens.reshape(TOKENS, D), grad_gates.reshape(TOKENS, TOPK)
```

```python
import jax
import jax.numpy as jnp
from jax import lax
from jax.experimental import pallas as pl
from jax.experimental.pallas import tpu as pltpu
from jax.sharding import PartitionSpec as P

CAP = 48
MESH = pl.DeviceIdType.MESH
F32 = jnp.float32
BF16 = jnp.bfloat16
NT = (((1,), (1,)), ((), ()))
TN = (((0,), (0,)), ((), ()))
ANTI = 7


def dot(a, b):
    return jnp.dot(a, b, preferred_element_type=F32)


def dot_nt(a, b):
    return lax.dot_general(a, b, NT, preferred_element_type=F32)


def dot_tn(a, b):
    return lax.dot_general(a, b, TN, preferred_element_type=F32)


def kernel(
    routes, gates, tok, grad, wg_hbm, wu_hbm, wd_hbm,
    mixed, grad_tokens, grad_gates_t,
    wg, wu, wd, ag, picked, act, scl, hid, gg, gu, pb, rs_rx, rs_tx,
    ret, ret_tx, pick_t, wm_t, ids_t, xs_tx, xs_rx, zacc, zs_tx, zs_rx, res,
    g_tx, g_rx, g_all,
    w_sem, ag_s, ag_r, rs_s, rs_r, pk_s, pk_r, rt_s, rt_r,
    xs_s, xs_r, zs_s, zs_r, za_s, za_r, xa_s, xa_r, g1_s, g1_r, g2_s, g2_r, g3_s, g3_r,
):
    y, t, e = lax.axis_index("dp"), lax.axis_index("tensor"), lax.axis_index("expert")
    n_dp = 8
    zh, core = t // 2, t % 2
    x, zl = e // 4, e % 4
    mirror = x * 4 + 3 - zl
    t1 = 2 * zh + 1 - core
    t2 = 2 * (1 - zh) + core
    t3 = 2 * (1 - zh) + 1 - core
    feats = (t, t1, t2, t3)
    experts = (4 * e + t, 4 * e + t1, 4 * mirror + t2, 4 * mirror + t3)
    peers = (None, (y, t1, e), (y, t2, mirror), (y, t3, mirror))
    up = (lax.rem(y + 1, n_dp), t, e)
    down = (lax.rem(y + n_dp - 1, n_dp), t, e)
    ring = (up, down)
    x_at = [lax.rem(x + rel, 4) for rel in range(4)]
    z_at = [lax.rem(zl + rel, 4) for rel in range(4)]
    x_peers = [(y, t, x_at[rel] * 4 + zl) for rel in range(4)]
    z_peers = [(y, t, x * 4 + z_at[rel]) for rel in range(4)]

    started = []

    def send(src, dst, s, r, to):
        copy = pltpu.make_async_remote_copy(
            src_ref=src, dst_ref=dst, send_sem=s, recv_sem=r, device_id=to, device_id_type=MESH
        )
        copy.start()
        started.append(copy)
        return copy

    loads = []
    for n, (hbm, vmem) in enumerate(((wg_hbm, wg), (wu_hbm, wu), (wd_hbm, wd))):
        for j in range(4):
            at = pl.multiple_of(feats[j] * 512, 512)
            load = pltpu.make_async_copy(hbm.at[0, :, pl.ds(at, 512)], vmem.at[j], w_sem.at[n, j])
            load.start()
            loads.append(load)

    barrier = pltpu.get_barrier_semaphore()
    everyone = list(ring) + list(peers[1:]) + x_peers[1:] + z_peers[1:]
    for peer in everyone:
        pl.semaphore_signal(barrier, inc=1, device_id=peer, device_id_type=MESH)

    eye = (
        lax.broadcasted_iota(jnp.int32, (8, 8), 0) == lax.broadcasted_iota(jnp.int32, (8, 8), 1)
    ).astype(F32).astype(BF16)
    ids = dot_nt(eye, routes[...].astype(F32).astype(BF16)).astype(jnp.int32)
    gate_rows = dot_nt(eye, gates[...].astype(BF16))
    ids_t[...] = ids
    row8 = lax.broadcasted_iota(jnp.int32, (8, 512), 0)
    masks = []
    chosen = jnp.zeros((8, 512), F32)
    for q in range(4):
        mask = jnp.sum((ids == experts[q]).astype(F32), axis=0, keepdims=True)
        masks.append(mask)
        chosen = chosen + jnp.where(row8 == q, mask, 0.0)
    before = (
        lax.broadcasted_iota(jnp.int32, (512, 512), 0) < lax.broadcasted_iota(jnp.int32, (512, 512), 1)
    ).astype(F32).astype(BF16)
    rank = dot(chosen.astype(BF16), before).astype(jnp.int32)
    slot = lax.broadcasted_iota(jnp.int32, (CAP, 512), 0)
    for q in range(4):
        hit = (slot == rank[q : q + 1]) & (masks[q] > 0.0)
        gate = jnp.sum(jnp.where(ids == experts[q], gate_rows, 0.0), axis=0, keepdims=True)
        pick_t[48 * q : 48 * q + 48] = jnp.where(hit, 1.0, 0.0).astype(BF16)
        wm_t[48 * q : 48 * q + 48] = jnp.where(hit, gate, 0.0).astype(BF16)

    ag_copy, pk_copy = {}, {}

    def ag_send(kind, way, d, j, src, dst):
        ag_copy[kind, way, d, j] = send(
            ag.at[kind, j, src], ag.at[kind, j, dst],
            ag_s.at[kind, way, d, j], ag_r.at[kind, way, d, j], ring[way],
        )

    def send_own(kind, j):
        ag_send(kind, 0, 0, j, 0, 1)
        ag_send(kind, 1, 0, j, 0, 2)

    for kind, rows in ((0, tok), (1, grad)):
        got = dot(pick_t[...], rows[...]).astype(BF16)
        ag[kind, 0, 0] = got[0:48]
        for q in (2, 3, 1):
            picked[kind, q - 1] = got[48 * q : 48 * q + 48]
        if kind == 0:
            pl.semaphore_wait(barrier, len(everyone))
        for q in (2, 3, 1):
            pk_copy[kind, q] = send(
                picked.at[kind, q - 1], ag.at[kind, q, 0], pk_s.at[kind, q - 1], pk_r.at[kind, q - 1], peers[q]
            )
        send_own(kind, 0)

    def own_in(kind, j):
        pk_copy[kind, j].wait_recv()
        send_own(kind, j)

    own_in(0, 1)
    own_in(1, 1)
    own_in(0, 2)
    own_in(0, 3)
    for load in loads:
        load.wait()

    def rows_of(kind, j, s0, n):
        return ag[kind, j, s0 : s0 + n].reshape(n * CAP, 512)

    tasks = []

    def forward(s0, n):
        def first():
            gate_pre = dot_nt(rows_of(0, 0, s0, n), wg[0])
            for j in range(1, 4):
                gate_pre = gate_pre + dot_nt(rows_of(0, j, s0, n), wg[j])
            sig = jax.nn.sigmoid(gate_pre)
            act[s0 : s0 + n] = (gate_pre * sig).reshape(n, CAP, 192)
            scl[s0 : s0 + n] = (sig * (1.0 + gate_pre * (1.0 - sig))).reshape(n, CAP, 192)

        def second():
            up_pre = dot_nt(rows_of(0, 0, s0, n), wu[0])
            for j in range(1, 4):
                up_pre = up_pre + dot_nt(rows_of(0, j, s0, n), wu[j])
            up_pre = up_pre.reshape(n, CAP, 192)
            hid[s0 : s0 + n] = (act[s0 : s0 + n] * up_pre).astype(BF16)
            scl[s0 : s0 + n] = up_pre * scl[s0 : s0 + n]

        def third(j):
            out = dot(hid[s0 : s0 + n].reshape(n * CAP, 192), wd[j])
            pb[0, s0 : s0 + n, j] = out.astype(BF16).reshape(n, CAP, 512)

        return [first, second] + [lambda j=j: third(j) for j in range(4)]

    def backward(s0, n):
        def first():
            grad_hid = dot_nt(rows_of(1, 0, s0, n), wd[0])
            for j in range(1, 4):
                grad_hid = grad_hid + dot_nt(rows_of(1, j, s0, n), wd[j])
            grad_hid = grad_hid.reshape(n, CAP, 192)
            gg[s0 : s0 + n] = (grad_hid * scl[s0 : s0 + n]).astype(BF16)
            gu[s0 : s0 + n] = (grad_hid * act[s0 : s0 + n]).astype(BF16)

        def second(j):
            back = dot(gg[s0 : s0 + n].reshape(n * CAP, 192), wg[j])
            back = back + dot(gu[s0 : s0 + n].reshape(n * CAP, 192), wu[j])
            pb[1, s0 : s0 + n, j] = back.astype(BF16).reshape(n, CAP, 512)

        return [first] + [lambda j=j: second(j) for j in range(4)]

    def work(n):
        for _ in range(min(n, len(tasks))):
            tasks.pop(0)()

    def gather(kind, make):
        for d in range(1, 5):
            for j in range(4):
                for way in range(2):
                    if d == 4 and (j < 2) != (way == 0):
                        continue
                    ag_copy[kind, way, d - 1, j].wait_recv()
                    if d < 3:
                        ag_send(kind, way, d, j, 2 * d - 1 + way, 2 * d + 1 + way)
                    elif d == 3 and (j < 2) == (way == 0):
                        ag_send(kind, way, d, j, 2 * d - 1 + way, ANTI)
                if kind == 1 and d == 3 and j == 3:
                    scatter_first(0)
                work(2)
            tasks.extend(make(2 * d - 1, 2) if d < 4 else make(ANTI, 1))

    rs_copy = {}

    def rs_send(kind, way, s, j, src):
        rs_copy[kind, way, s, j] = send(
            src, rs_rx.at[kind, way, s, j], rs_s.at[kind, way, s, j], rs_r.at[kind, way, s, j], ring[way]
        )

    def scatter_first(kind):
        for j in range(2):
            rs_send(kind, 0, 0, j, pb.at[kind, ANTI, j])
            rs_send(kind, 1, 0, j + 2, pb.at[kind, ANTI, j + 2])

    def scatter(kind, s, busy):
        d = 4 - s
        for j in range(4):
            for way in range(2):
                at = 2 * d if way == 0 else 2 * d - 1
                if s == 1 and (j < 2) != (way == 0):
                    rs_send(kind, way, s, j, pb.at[kind, at, j])
                    continue
                rs_copy[kind, way, s - 1, j].wait_recv()
                rs_tx[kind, way, s - 1, j] = (
                    pb[kind, at, j].astype(F32) + rs_rx[kind, way, s - 1, j].astype(F32)
                ).astype(BF16)
                rs_send(kind, way, s, j, rs_tx.at[kind, way, s - 1, j])
            work(busy)

    rt_copy = {}

    def home(kind):
        products = None
        for j in (2, 3, 1, 0):
            for way in range(2):
                rs_copy[kind, way, 3, j].wait_recv()
            total = (
                pb[kind, 0, j].astype(F32)
                + rs_rx[kind, 0, 3, j].astype(F32)
                + rs_rx[kind, 1, 3, j].astype(F32)
            ).astype(BF16)
            if j == 0:
                ret[kind, 0:48] = total
            else:
                ret_tx[kind, j - 1] = total
                rt_copy[kind, j] = send(
                    ret_tx.at[kind, j - 1], ret.at[kind, pl.ds(48 * j, 48)],
                    rt_s.at[kind, j - 1], rt_r.at[kind, j - 1], peers[j],
                )
            if kind == 0:
                term = jnp.sum(total.astype(F32) * ag[1, j, 0].astype(F32), axis=1, keepdims=True)
                products = term if products is None else products + term
        if kind == 0:
            own = jnp.sum(pick_t[0:48].astype(F32) * products, axis=0, keepdims=True)
            g_tx[0] = jnp.broadcast_to(own, (8, 512))
            for j in (2, 3, 1):
                g_copy[1, j] = send(g_tx.at[0], g_rx.at[j - 1], g1_s.at[j - 1], g1_r.at[j - 1], peers[j])

    g_copy, e_copy = {}, {}

    def gates_second():
        block = jnp.where(row8 == 0, g_tx[0], 0.0)
        for j in range(1, 4):
            g_copy[1, j].wait_recv()
            block = block + jnp.where(row8 == j, g_rx[j - 1], 0.0)
        g_tx[1] = block
        g_all[zl, x] = block
        for rel in range(1, 4):
            g_copy[2, rel] = send(
                g_tx.at[1], g_all.at[zl, x], g2_s.at[rel - 1], g2_r.at[rel - 1], x_peers[rel]
            )

    def gates_third():
        for rel in range(1, 4):
            g_copy[2, rel].wait_recv()
        for rel in range(1, 4):
            g_copy[3, rel] = send(
                g_all.at[zl], g_all.at[zl], g3_s.at[rel - 1], g3_r.at[rel - 1], z_peers[rel]
            )

    def gates_last():
        for rel in range(1, 4):
            g_copy[3, rel].wait_recv()
        ids_now = ids_t[...]
        sums = [jnp.zeros((8, 512), F32) for _ in range(8)]
        for zz in range(4):
            for xx in range(4):
                there, opposite = 4 * (xx * 4 + zz), 4 * (xx * 4 + 3 - zz)
                names = jnp.where(row8 == 0, there + t, -1)
                names = jnp.where(row8 == 1, there + t1, names)
                names = jnp.where(row8 == 2, opposite + t2, names)
                names = jnp.where(row8 == 3, opposite + t3, names)
                block = g_all[zz, xx]
                for r in range(8):
                    sums[r] = sums[r] + jnp.where(ids_now[r : r + 1] == names, block, 0.0)
        for r in range(8):
            grad_gates_t[r : r + 1] = jnp.sum(sums[r], axis=0, keepdims=True)

    def cols(at):
        return pl.ds(pl.multiple_of(at * 128, 128), 128)

    def x_scatter(kind):
        for j in range(1, 4):
            rt_copy[kind, j].wait_recv()
        for rel in (2, 1, 3):
            part = dot_tn(wm_t[:, cols(x_at[rel])], ret[kind])
            xs_tx[kind, rel - 1] = part.astype(BF16)
            e_copy["xs", kind, rel] = send(
                xs_tx.at[kind, rel - 1], xs_rx.at[kind, rel - 1],
                xs_s.at[kind, rel - 1], xs_r.at[kind, rel - 1], x_peers[rel],
            )
        zacc[kind] = dot_tn(wm_t[:, cols(x)], ret[kind])

    def z_scatter(kind):
        for rel in (1, 3, 2):
            e_copy["xs", kind, rel].wait_recv()
        total = zacc[kind]
        for rel in range(1, 4):
            total = total + xs_rx[kind, rel - 1].astype(F32)
        zacc[kind] = total
        zs_tx[kind] = total.astype(BF16)
        for rel in (2, 1, 3):
            rows = pl.ds(pl.multiple_of(z_at[rel] * 32, 32), 32)
            e_copy["zs", kind, rel] = send(
                zs_tx.at[kind, rows], zs_rx.at[kind, rel - 1],
                zs_s.at[kind, rel - 1], zs_r.at[kind, rel - 1], z_peers[rel],
            )

    def z_gather(kind):
        total = zacc[kind, pl.ds(pl.multiple_of(zl * 32, 32), 32)]
        for rel in (1, 3, 2):
            e_copy["zs", kind, rel].wait_recv()
        for rel in range(1, 4):
            total = total + zs_rx[kind, rel - 1].astype(F32)
        rows = pl.ds(pl.multiple_of(x * 128 + zl * 32, 32), 32)
        res[kind, rows] = total.astype(BF16)
        for rel in (2, 1, 3):
            e_copy["za", kind, rel] = send(
                res.at[kind, rows], res.at[kind, rows],
                za_s.at[kind, rel - 1], za_r.at[kind, rel - 1], z_peers[rel],
            )

    def x_gather(kind):
        for rel in (1, 3, 2):
            e_copy["za", kind, rel].wait_recv()
        rows = pl.ds(pl.multiple_of(x * 128, 128), 128)
        for rel in (2, 1, 3):
            e_copy["xa", kind, rel] = send(
                res.at[kind, rows], res.at[kind, rows],
                xa_s.at[kind, rel - 1], xa_r.at[kind, rel - 1], x_peers[rel],
            )

    def finish(kind, out):
        for rel in (1, 3, 2):
            e_copy["xa", kind, rel].wait_recv()
        out[...] = res[kind]

    tasks.extend(forward(0, 1))
    gather(0, forward)
    own_in(1, 2)
    own_in(1, 3)
    tasks.extend(backward(0, 1))
    gather(1, backward)
    for s in range(1, 4):
        scatter(0, s, 2)
    work(len(tasks))
    scatter_first(1)
    home(0)
    scatter(1, 1, 0)
    x_scatter(0)
    gates_second()
    scatter(1, 2, 0)
    z_scatter(0)
    gates_third()
    scatter(1, 3, 0)
    z_gather(0)
    home(1)
    x_gather(0)
    x_scatter(1)
    gates_last()
    z_scatter(1)
    finish(0, mixed)
    z_gather(1)
    x_gather(1)
    finish(1, grad_tokens)
    for copy in started:
        copy.wait_send()


def body(tokens, grad_out, routes, gates, gate_weight, up_weight, down_weight):
    vmem = pl.BlockSpec(memory_space=pltpu.VMEM)
    anywhere = pl.BlockSpec(memory_space=pl.ANY)
    dma = pltpu.SemaphoreType.DMA
    mixed, grad_tokens, grad_gates_t = pl.pallas_call(
        kernel,
        out_shape=(
            jax.ShapeDtypeStruct((512, 512), BF16),
            jax.ShapeDtypeStruct((512, 512), BF16),
            jax.ShapeDtypeStruct((8, 512), F32),
        ),
        in_specs=[vmem] * 4 + [anywhere] * 3,
        out_specs=(vmem, vmem, vmem),
        scratch_shapes=[
            pltpu.VMEM((4, 192, 512), BF16),
            pltpu.VMEM((4, 192, 512), BF16),
            pltpu.VMEM((4, 192, 512), BF16),
            pltpu.VMEM((2, 4, 8, CAP, 512), BF16),
            pltpu.VMEM((2, 3, CAP, 512), BF16),
            pltpu.VMEM((8, CAP, 192), F32),
            pltpu.VMEM((8, CAP, 192), F32),
            pltpu.VMEM((8, CAP, 192), BF16),
            pltpu.VMEM((8, CAP, 192), BF16),
            pltpu.VMEM((8, CAP, 192), BF16),
            pltpu.VMEM((2, 8, 4, CAP, 512), BF16),
            pltpu.VMEM((2, 2, 4, 4, CAP, 512), BF16),
            pltpu.VMEM((2, 2, 3, 4, CAP, 512), BF16),
            pltpu.VMEM((2, 192, 512), BF16),
            pltpu.VMEM((2, 3, CAP, 512), BF16),
            pltpu.VMEM((192, 512), BF16),
            pltpu.VMEM((192, 512), BF16),
            pltpu.VMEM((8, 512), jnp.int32),
            pltpu.VMEM((2, 3, 128, 512), BF16),
            pltpu.VMEM((2, 3, 128, 512), BF16),
            pltpu.VMEM((2, 128, 512), F32),
            pltpu.VMEM((2, 128, 512), BF16),
            pltpu.VMEM((2, 3, 32, 512), BF16),
            pltpu.VMEM((2, 512, 512), BF16),
            pltpu.VMEM((2, 8, 512), F32),
            pltpu.VMEM((3, 8, 512), F32),
            pltpu.VMEM((4, 4, 8, 512), F32),
            dma((3, 4)),
            dma((2, 2, 4, 4)),
            dma((2, 2, 4, 4)),
            dma((2, 2, 4, 4)),
            dma((2, 2, 4, 4)),
            dma((2, 3)),
            dma((2, 3)),
            dma((2, 3)),
            dma((2, 3)),
            dma((2, 3)),
            dma((2, 3)),
            dma((2, 3)),
            dma((2, 3)),
            dma((2, 3)),
            dma((2, 3)),
            dma((2, 3)),
            dma((2, 3)),
            dma((3,)),
            dma((3,)),
            dma((3,)),
            dma((3,)),
            dma((3,)),
            dma((3,)),
        ],
        compiler_params=pltpu.CompilerParams(
            collective_id=0, has_side_effects=True, vmem_limit_bytes=48 * 1024 * 1024
        ),
    )(routes, gates, tokens, grad_out, gate_weight, up_weight, down_weight)
    return mixed, grad_tokens, grad_gates_t.T


def solution(mesh):
    return jax.shard_map(
        body,
        mesh=mesh,
        in_specs=(
            P("dp", "tensor"),
            P("dp", "tensor"),
            P("dp", None),
            P("dp", None),
            P(("expert", "tensor"), "dp", None),
            P(("expert", "tensor"), "dp", None),
            P(("expert", "tensor"), "dp", None),
        ),
        out_specs=(P("dp", "tensor"), P("dp", "tensor"), P("dp", None)),
        check_vma=False,
    )
```

```python
import jax
import jax.numpy as jnp
from jax import lax
from jax.experimental import pallas as pl
from jax.experimental.pallas import tpu as pltpu
from jax.sharding import PartitionSpec as P

CAP = 48
MESH = pl.DeviceIdType.MESH
F32 = jnp.float32
BF16 = jnp.bfloat16
NT = (((1,), (1,)), ((), ()))
ANTI = 7


def dot(a, b):
    return jnp.dot(a, b, preferred_element_type=F32)


def dot_nt(a, b):
    return lax.dot_general(a, b, NT, preferred_element_type=F32)


def kernel(
    routes, gates, tok_hbm, grad_hbm, wg_hbm, wu_hbm, wd_hbm,
    mixed, grad_tokens, grad_gates_t,
    rows_in, wg, wu, wd, ag, picked, sums, act, scl, hid, gg, gu, pb, rs_rx, rs_tx,
    ret, ret_tx, pick_t, wm_t, wm, xs_tx, xs_rx, zacc, zs_tx, zs_rx,
    g_tx, g_rx, g_all,
    w_sem, in_sem, ag_s, ag_r, rs_s, rs_r, pk_s, pk_r, rt_s, rt_r,
    xs_s, xs_r, zs_s, zs_r, za_s, za_r, xa_s, xa_r, g1_s, g1_r, g2_s, g2_r, g3_s, g3_r,
):
    y, t, e = lax.axis_index("dp"), lax.axis_index("tensor"), lax.axis_index("expert")
    n_dp = 8
    zh, core = t // 2, t % 2
    x, zl = e // 4, e % 4
    mirror = x * 4 + 3 - zl
    t1 = 2 * zh + 1 - core
    t2 = 2 * (1 - zh) + core
    t3 = 2 * (1 - zh) + 1 - core
    feats = (t, t1, t2, t3)
    experts = (4 * e + t, 4 * e + t1, 4 * mirror + t2, 4 * mirror + t3)
    peers = (None, (y, t1, e), (y, t2, mirror), (y, t3, mirror))
    up = (lax.rem(y + 1, n_dp), t, e)
    down = (lax.rem(y + n_dp - 1, n_dp), t, e)
    ring = (up, down)
    x_at = [lax.rem(x + rel, 4) for rel in range(4)]
    z_at = [lax.rem(zl + rel, 4) for rel in range(4)]
    x_peers = [(y, t, x_at[rel] * 4 + zl) for rel in range(4)]
    z_peers = [(y, t, x * 4 + z_at[rel]) for rel in range(4)]
    results = (mixed, grad_tokens)

    started = []

    def send(src, dst, s, r, to):
        copy = pltpu.make_async_remote_copy(
            src_ref=src, dst_ref=dst, send_sem=s, recv_sem=r, device_id=to, device_id_type=MESH
        )
        copy.start()
        started.append(copy)
        return copy

    barrier = pltpu.get_barrier_semaphore()
    everyone = list(ring) + list(peers[1:]) + x_peers[1:] + z_peers[1:]
    for peer in everyone:
        pl.semaphore_signal(barrier, inc=1, device_id=peer, device_id_type=MESH)

    row_loads = []
    for kind, hbm in enumerate((tok_hbm, grad_hbm)):
        load = pltpu.make_async_copy(hbm, rows_in.at[kind], in_sem.at[kind])
        load.start()
        row_loads.append(load)

    loads = []
    for n, (hbm, vmem) in enumerate(((wg_hbm, wg), (wu_hbm, wu), (wd_hbm, wd))):
        for j in range(4):
            at = pl.multiple_of(feats[j] * 512, 512)
            load = pltpu.make_async_copy(hbm.at[0, :, pl.ds(at, 512)], vmem.at[j], w_sem.at[n, j])
            load.start()
            loads.append(load)

    ids = routes[...]
    gate_rows = gates[...]
    row8 = lax.broadcasted_iota(jnp.int32, (8, 512), 0)
    masks = []
    chosen = jnp.zeros((8, 512), F32)
    for q in range(4):
        mask = jnp.sum((ids == experts[q]).astype(F32), axis=0, keepdims=True)
        masks.append(mask)
        chosen = chosen + jnp.where(row8 == q, mask, 0.0)
    rows512 = lax.broadcasted_iota(jnp.int32, (512, 512), 0)
    cols512 = lax.broadcasted_iota(jnp.int32, (512, 512), 1)
    before = (rows512 < cols512).astype(F32).astype(BF16)
    rank = dot(chosen.astype(BF16), before).astype(jnp.int32)
    slot = lax.broadcasted_iota(jnp.int32, (CAP, 512), 0)
    for q in range(4):
        hit = (slot == rank[q : q + 1]) & (masks[q] > 0.0)
        gate = jnp.sum(jnp.where(ids == experts[q], gate_rows, 0.0), axis=0, keepdims=True)
        pick_t[48 * q : 48 * q + 48] = jnp.where(hit, 1.0, 0.0).astype(BF16)
        wm_t[48 * q : 48 * q + 48] = jnp.where(hit, gate, 0.0).astype(BF16)

    ag_copy, pk_copy = {}, {}

    def ag_send(kind, way, d, j, src, dst):
        ag_copy[kind, way, d, j] = send(
            ag.at[kind, j, src], ag.at[kind, j, dst],
            ag_s.at[kind, way, d, j], ag_r.at[kind, way, d, j], ring[way],
        )

    def send_own(kind, j):
        ag_send(kind, 0, 0, j, 0, 1)
        ag_send(kind, 1, 0, j, 0, 2)

    for kind in range(2):
        row_loads[kind].wait()
        got = dot(pick_t[...], rows_in[kind]).astype(BF16)
        ag[kind, 0, 0] = got[0:48]
        for q in (2, 3, 1):
            picked[kind, q - 1] = got[48 * q : 48 * q + 48]
        if kind == 0:
            pl.semaphore_wait(barrier, len(everyone))
        for q in (1, 2, 3):
            pk_copy[kind, q] = send(
                picked.at[kind, q - 1], ag.at[kind, q, 0], pk_s.at[kind, q - 1], pk_r.at[kind, q - 1], peers[q]
            )
        send_own(kind, 0)

    def own_in(kind, j):
        pk_copy[kind, j].wait_recv()
        send_own(kind, j)

    own_in(0, 1)
    own_in(1, 1)
    for load in loads:
        load.wait()

    def rows_of(kind, j, s0, n):
        return ag[kind, j, s0 : s0 + n].reshape(n * CAP, 512)

    def half_sum(kind, w, j, s0, n):
        both = dot_nt(rows_of(kind, j, s0, n), w[j]) + dot_nt(rows_of(kind, j + 1, s0, n), w[j + 1])
        return both.reshape(n, CAP, 192)

    urgent, later = [], []

    def early(s0, n):
        def one(i, kind, w):
            sums[i, s0 : s0 + n] = half_sum(kind, w, 0, s0, n)

        return [lambda i=i, k=k, w=w: one(i, k, w) for i, (k, w) in enumerate(((0, wg), (0, wu), (1, wd)))]

    def forward(s0, n):
        def first():
            gate_pre = sums[0, s0 : s0 + n] + half_sum(0, wg, 2, s0, n)
            sig = jax.nn.sigmoid(gate_pre)
            act[s0 : s0 + n] = gate_pre * sig
            scl[s0 : s0 + n] = sig * (1.0 + gate_pre * (1.0 - sig))

        def second():
            up_pre = sums[1, s0 : s0 + n] + half_sum(0, wu, 2, s0, n)
            hid[s0 : s0 + n] = (act[s0 : s0 + n] * up_pre).astype(BF16)
            scl[s0 : s0 + n] = up_pre * scl[s0 : s0 + n]

        def third(j):
            out = dot(hid[s0 : s0 + n].reshape(n * CAP, 192), wd[j]).astype(BF16)
            for h in range(2):
                pb[0, h, s0 : s0 + n, j] = out[:, 256 * h : 256 * h + 256].reshape(n, CAP, 256)

        return [first, second] + [lambda j=j: third(j) for j in range(4)]

    def backward(s0, n):
        def first():
            grad_hid = sums[2, s0 : s0 + n] + half_sum(1, wd, 2, s0, n)
            gg[s0 : s0 + n] = (grad_hid * scl[s0 : s0 + n]).astype(BF16)
            gu[s0 : s0 + n] = (grad_hid * act[s0 : s0 + n]).astype(BF16)

        def second(j):
            back = dot(gg[s0 : s0 + n].reshape(n * CAP, 192), wg[j])
            back = back + dot(gu[s0 : s0 + n].reshape(n * CAP, 192), wu[j])
            back = back.astype(BF16)
            for h in range(2):
                pb[1, h, s0 : s0 + n, j] = back[:, 256 * h : 256 * h + 256].reshape(n, CAP, 256)

        return [first] + [lambda j=j: second(j) for j in range(4)]

    def work(n):
        for _ in range(min(n, len(urgent) + len(later))):
            (urgent or later).pop(0)()

    def span(d):
        return (2 * d - 1, 2) if d < 4 else (ANTI, 1)

    def arrive(kind, d, j):
        for way in range(2):
            if d == 4 and j % 2 != way:
                continue
            ag_copy[kind, way, d - 1, j].wait_recv()
            if d < 3:
                ag_send(kind, way, d, j, 2 * d - 1 + way, 2 * d + 1 + way)
            elif d == 3 and j % 2 == way:
                ag_send(kind, way, d, j, 2 * d - 1 + way, ANTI)

    urgent.extend(early(0, 1))
    for d in range(1, 5):
        for kind in range(2):
            for j in range(2):
                arrive(kind, d, j)
                work(1)
            if d == 4:
                own_in(kind, 2)
                own_in(kind, 3)
        urgent.extend(early(*span(d)))

    rs_copy = {}

    def rs_send(u, way, s, p, src):
        kind, h = u
        rs_copy[u, way, s, p] = send(
            src, rs_rx.at[kind, h, way, s, pl.ds(2 * p, 2)],
            rs_s.at[kind, h, way, s, p], rs_r.at[kind, h, way, s, p], ring[way],
        )

    def first(u):
        for way in range(2):
            rs_send(u, way, 0, way, pb.at[u[0], u[1], ANTI, pl.ds(2 * way, 2)])

    def free(u):
        for way in range(2):
            rs_send(u, way, 1, 1 - way, pb.at[u[0], u[1], 6 - way, pl.ds(2 - 2 * way, 2)])

    def add_on(u, s, turn):
        kind, h = u
        d = 4 - s
        for way in range(2):
            p = 1 - way if turn == 0 else way
            at, js = 2 * d - way, slice(2 * p, 2 * p + 2)
            rs_copy[u, way, s - 1, p].wait_recv()
            rs_tx[kind, h, way, s - 1, js] = (
                pb[kind, h, at, js].astype(F32) + rs_rx[kind, h, way, s - 1, js].astype(F32)
            ).astype(BF16)
        for way in range(2):
            p = 1 - way if turn == 0 else way
            rs_send(u, way, s, p, rs_tx.at[kind, h, way, s - 1, pl.ds(2 * p, 2)])

    def scatter(u, s):
        if s > 1:
            add_on(u, s, 0)
            work(2)
        add_on(u, s, 1)
        work(2)

    u0, u1, u2, u3 = (0, 0), (0, 1), (1, 0), (1, 1)

    urgent.extend(forward(0, 1))
    for d in range(1, 5):
        for j in (2, 3):
            arrive(0, d, j)
            work(4)
        if d == 1:
            later.extend(backward(0, 1))
        if d == 4:
            work(len(urgent))
            urgent.extend(forward(*span(d)))
            work(len(urgent))
            first(u0)
        else:
            urgent.extend(forward(*span(d)))
        for j in (2, 3):
            arrive(1, d, j)
            work(4)
        if d == 3:
            work(len(urgent))
            free(u0)
            free(u1)
        later.extend(backward(*span(d)))

    rt_copy, g_copy, e_copy = {}, {}, {}
    products = []

    def home(u):
        kind, h = u
        for p in (1, 0):
            for way in range(2):
                rs_copy[u, way, 3, p].wait_recv()
            for j in (2 * p + 1, 2 * p):
                total = (
                    pb[kind, h, 0, j].astype(F32)
                    + rs_rx[kind, h, 0, 3, j].astype(F32)
                    + rs_rx[kind, h, 1, 3, j].astype(F32)
                ).astype(BF16)
                if j == 0:
                    ret[kind, h, 0:48] = total
                else:
                    ret_tx[kind, h, j - 1] = total
                if kind == 0:
                    theirs = ag[1, j, 0, :, 256 * h : 256 * h + 256].astype(F32)
                    products.append(jnp.sum(total.astype(F32) * theirs, axis=1, keepdims=True))
            for j in (2 * p + 1, 2 * p):
                if j:
                    rt_copy[u, j] = send(
                        ret_tx.at[kind, h, j - 1], ret.at[kind, h, pl.ds(48 * j, 48)],
                        rt_s.at[kind, h, j - 1], rt_r.at[kind, h, j - 1], peers[j],
                    )

    def gates_first():
        total = products[0]
        for term in products[1:]:
            total = total + term
        own = jnp.sum(pick_t[0:48].astype(F32) * total, axis=0, keepdims=True)
        g_tx[0] = jnp.broadcast_to(own, (8, 512))
        for j in (2, 3, 1):
            g_copy[1, j] = send(g_tx.at[0], g_rx.at[j - 1], g1_s.at[j - 1], g1_r.at[j - 1], peers[j])

    def gates_second():
        block = jnp.where(row8 == 0, g_tx[0], 0.0)
        for j in range(1, 4):
            g_copy[1, j].wait_recv()
            block = block + jnp.where(row8 == j, g_rx[j - 1], 0.0)
        g_tx[1] = block
        g_all[zl, x] = block
        for rel in range(1, 4):
            g_copy[2, rel] = send(
                g_tx.at[1], g_all.at[zl, x], g2_s.at[rel - 1], g2_r.at[rel - 1], x_peers[rel]
            )

    def gates_third():
        for rel in range(1, 4):
            g_copy[2, rel].wait_recv()
        for rel in range(1, 4):
            g_copy[3, rel] = send(
                g_all.at[zl], g_all.at[zl], g3_s.at[rel - 1], g3_r.at[rel - 1], z_peers[rel]
            )

    def gates_last():
        for rel in range(1, 4):
            g_copy[3, rel].wait_recv()
        ids_now = routes[...]
        totals = [jnp.zeros((8, 512), F32) for _ in range(8)]
        for zz in range(4):
            for xx in range(4):
                there, opposite = 4 * (xx * 4 + zz), 4 * (xx * 4 + 3 - zz)
                names = jnp.where(row8 == 0, there + t, -1)
                names = jnp.where(row8 == 1, there + t1, names)
                names = jnp.where(row8 == 2, opposite + t2, names)
                names = jnp.where(row8 == 3, opposite + t3, names)
                block = g_all[zz, xx]
                for r in range(8):
                    totals[r] = totals[r] + jnp.where(ids_now[r : r + 1] == names, block, 0.0)
        for r in range(8):
            grad_gates_t[r : r + 1] = jnp.sum(totals[r], axis=0, keepdims=True)

    def x_scatter(u):
        kind, h = u
        for j in (1, 2, 3):
            rt_copy[u, j].wait_recv()
        for rel in (2, 1, 3):
            rows = pl.ds(pl.multiple_of(x_at[rel] * 128, 128), 128)
            xs_tx[kind, h, rel - 1] = dot(wm[rows], ret[kind, h]).astype(BF16)
            e_copy["xs", u, rel] = send(
                xs_tx.at[kind, h, rel - 1], xs_rx.at[kind, h, rel - 1],
                xs_s.at[kind, h, rel - 1], xs_r.at[kind, h, rel - 1], x_peers[rel],
            )
        zacc[kind, h] = dot(wm[pl.ds(pl.multiple_of(x * 128, 128), 128)], ret[kind, h])

    def z_scatter(u):
        kind, h = u
        for rel in (1, 3, 2):
            e_copy["xs", u, rel].wait_recv()
        total = zacc[kind, h]
        for rel in range(1, 4):
            total = total + xs_rx[kind, h, rel - 1].astype(F32)
        zacc[kind, h] = total
        zs_tx[kind, h] = total.astype(BF16)
        for rel in (2, 1, 3):
            rows = pl.ds(pl.multiple_of(z_at[rel] * 32, 32), 32)
            e_copy["zs", u, rel] = send(
                zs_tx.at[kind, h, rows], zs_rx.at[kind, h, rel - 1],
                zs_s.at[kind, h, rel - 1], zs_r.at[kind, h, rel - 1], z_peers[rel],
            )

    def z_gather(u):
        kind, h = u
        total = zacc[kind, h, pl.ds(pl.multiple_of(zl * 32, 32), 32)]
        for rel in (1, 3, 2):
            e_copy["zs", u, rel].wait_recv()
        for rel in range(1, 4):
            total = total + zs_rx[kind, h, rel - 1].astype(F32)
        rows = pl.ds(pl.multiple_of(x * 128 + zl * 32, 32), 32)
        out = results[kind]
        out[rows, 256 * h : 256 * h + 256] = total.astype(BF16)
        place = out.at[rows, pl.ds(256 * h, 256)]
        for rel in (2, 1, 3):
            e_copy["za", u, rel] = send(
                place, place, za_s.at[kind, h, rel - 1], za_r.at[kind, h, rel - 1], z_peers[rel]
            )

    def x_gather(u):
        kind, h = u
        for rel in (1, 3, 2):
            e_copy["za", u, rel].wait_recv()
        rows = pl.ds(pl.multiple_of(x * 128, 128), 128)
        place = results[kind].at[rows, pl.ds(256 * h, 256)]
        for rel in (2, 1, 3):
            e_copy["xa", u, rel] = send(
                place, place, xa_s.at[kind, h, rel - 1], xa_r.at[kind, h, rel - 1], x_peers[rel]
            )

    def finish(u):
        for rel in (1, 3, 2):
            e_copy["xa", u, rel].wait_recv()

    wm[...] = dot_nt((rows512 == cols512).astype(F32).astype(BF16), wm_t[...]).astype(BF16)
    first(u1)
    scatter(u0, 1)
    scatter(u1, 1)
    scatter(u0, 2)
    work(len(urgent) + len(later))
    free(u2)
    free(u3)
    scatter(u0, 3)
    first(u2)
    scatter(u1, 2)
    home(u0)
    scatter(u1, 3)
    scatter(u2, 1)
    x_scatter(u0)
    first(u3)
    scatter(u2, 2)
    home(u1)
    scatter(u2, 3)
    gates_first()
    scatter(u3, 1)
    z_scatter(u0)
    x_scatter(u1)
    scatter(u3, 2)
    z_gather(u0)
    home(u2)
    scatter(u3, 3)
    gates_second()
    z_scatter(u1)
    x_scatter(u2)
    x_gather(u0)
    home(u3)
    gates_third()
    z_gather(u1)
    z_scatter(u2)
    x_scatter(u3)
    x_gather(u1)
    z_gather(u2)
    gates_last()
    z_scatter(u3)
    x_gather(u2)
    z_gather(u3)
    x_gather(u3)
    for u in (u0, u1, u2, u3):
        finish(u)
    for copy in started:
        copy.wait_send()


def body(tokens, grad_out, routes, gates, gate_weight, up_weight, down_weight):
    vmem = pl.BlockSpec(memory_space=pltpu.VMEM)
    hbm = pl.BlockSpec(memory_space=pltpu.HBM)
    dma = pltpu.SemaphoreType.DMA
    mixed, grad_tokens, grad_gates_t = pl.pallas_call(
        kernel,
        out_shape=(
            jax.ShapeDtypeStruct((512, 512), BF16),
            jax.ShapeDtypeStruct((512, 512), BF16),
            jax.ShapeDtypeStruct((8, 512), F32),
        ),
        in_specs=[vmem] * 2 + [hbm] * 5,
        out_specs=(vmem, vmem, vmem),
        scratch_shapes=[
            pltpu.VMEM((2, 512, 512), BF16),
            pltpu.VMEM((4, 192, 512), BF16),
            pltpu.VMEM((4, 192, 512), BF16),
            pltpu.VMEM((4, 192, 512), BF16),
            pltpu.VMEM((2, 4, 8, CAP, 512), BF16),
            pltpu.VMEM((2, 3, CAP, 512), BF16),
            pltpu.VMEM((3, 8, CAP, 192), F32),
            pltpu.VMEM((8, CAP, 192), F32),
            pltpu.VMEM((8, CAP, 192), F32),
            pltpu.VMEM((8, CAP, 192), BF16),
            pltpu.VMEM((8, CAP, 192), BF16),
            pltpu.VMEM((8, CAP, 192), BF16),
            pltpu.VMEM((2, 2, 8, 4, CAP, 256), BF16),
            pltpu.VMEM((2, 2, 2, 4, 4, CAP, 256), BF16),
            pltpu.VMEM((2, 2, 2, 3, 4, CAP, 256), BF16),
            pltpu.VMEM((2, 2, 192, 256), BF16),
            pltpu.VMEM((2, 2, 3, CAP, 256), BF16),
            pltpu.VMEM((192, 512), BF16),
            pltpu.VMEM((192, 512), BF16),
            pltpu.VMEM((512, 192), BF16),
            pltpu.VMEM((2, 2, 3, 128, 256), BF16),
            pltpu.VMEM((2, 2, 3, 128, 256), BF16),
            pltpu.VMEM((2, 2, 128, 256), F32),
            pltpu.VMEM((2, 2, 128, 256), BF16),
            pltpu.VMEM((2, 2, 3, 32, 256), BF16),
            pltpu.VMEM((2, 8, 512), F32),
            pltpu.VMEM((3, 8, 512), F32),
            pltpu.VMEM((4, 4, 8, 512), F32),
            dma((3, 4)),
            dma((2,)),
            dma((2, 2, 4, 4)),
            dma((2, 2, 4, 4)),
            dma((2, 2, 2, 4, 2)),
            dma((2, 2, 2, 4, 2)),
            dma((2, 3)),
            dma((2, 3)),
        ]
        + [dma((2, 2, 3))] * 10
        + [dma((3,))] * 6,
        compiler_params=pltpu.CompilerParams(
            collective_id=0, has_side_effects=True, vmem_limit_bytes=60500000
        ),
    )(routes.T, gates.T, tokens, grad_out, gate_weight, up_weight, down_weight)
    return mixed, grad_tokens, grad_gates_t.T


def solution(mesh):
    return jax.shard_map(
        body,
        mesh=mesh,
        in_specs=(
            P("dp", "tensor"),
            P("dp", "tensor"),
            P("dp", None),
            P("dp", None),
            P(("expert", "tensor"), "dp", None),
            P(("expert", "tensor"), "dp", None),
            P(("expert", "tensor"), "dp", None),
        ),
        out_specs=(P("dp", "tensor"), P("dp", "tensor"), P("dp", None)),
        check_vma=False,
    )
```

```python
import jax
import jax.numpy as jnp
from jax import lax
from jax.experimental import pallas as pl
from jax.experimental.pallas import tpu as pltpu
from jax.sharding import PartitionSpec as P

CAP = 48
MESH = pl.DeviceIdType.MESH
F32 = jnp.float32
BF16 = jnp.bfloat16
NT = (((1,), (1,)), ((), ()))
ANTI = 7
UNITS = ((0, 0, 0, 256), (0, 1, 0, 256), (1, 0, 0, 256), (1, 1, 0, 128), (1, 1, 128, 128))
PLAN = (
    ("ag", 0, 0, 1), ("E", 0, 0), ("E", 1, 0), ("ag", 0, 1, 0), ("ag", 1, 0, 1), ("E", 2, 0),
    ("ag", 1, 1, 0), ("ag", 0, 1, 1), ("E", 0, 1), ("E", 1, 1), ("ag", 0, 2, 0), ("ag", 0, 0, 2),
    ("F", 0), ("ag", 0, 0, 3), ("G", 0), ("P", 0, 0, 0), ("P", 0, 0, 1), ("P", 0, 0, 2),
    ("ag", 1, 1, 1), ("P", 0, 0, 3), ("E", 2, 1), ("E", 0, 2), ("ag", 0, 2, 1), ("E", 1, 2),
    ("ag", 0, 3, 0), ("B", 0), ("P", 1, 0, 0), ("ag", 1, 0, 2), ("P", 1, 0, 1), ("P", 1, 0, 2),
    ("P", 1, 0, 3), ("ag", 0, 1, 2), ("F", 1), ("G", 1), ("P", 0, 1, 0), ("ag", 0, 1, 3),
    ("P", 0, 1, 1), ("P", 0, 1, 2), ("P", 0, 1, 3), ("E", 2, 2), ("ag", 1, 0, 3), ("E", 0, 3),
    ("E", 1, 3), ("ag", 0, 3, 1), ("ag", 1, 2, 0), ("ag", 1, 1, 2), ("ag", 0, 2, 2), ("F", 2),
    ("G", 2), ("P", 0, 2, 0), ("ag", 0, 2, 3), ("P", 0, 2, 1), ("P", 0, 2, 2), ("P", 0, 2, 3),
    ("E", 0, 4), ("ag", 1, 1, 3), ("E", 1, 4), ("B", 1), ("P", 1, 1, 0), ("ag", 1, 2, 1),
    ("P", 1, 1, 1), ("P", 1, 1, 2), ("P", 1, 1, 3), ("ag", 1, 2, 2), ("ag", 0, 3, 2),
    ("ag", 1, 3, 0), ("F", 3), ("ag", 0, 3, 3), ("G", 3), ("P", 0, 3, 0), ("P", 0, 3, 1),
    ("ag", 1, 2, 3), ("P", 0, 3, 2), ("P", 0, 3, 3), ("free", 0), ("B", 2), ("E", 2, 3),
    ("P", 1, 2, 0), ("P", 1, 2, 1), ("free", 1), ("P", 1, 2, 2), ("P", 1, 2, 3), ("ag", 1, 3, 1),
    ("ag", 1, 3, 2), ("F", 4), ("G", 4), ("P", 0, 4, 0), ("P", 0, 4, 1), ("ag", 1, 3, 3),
    ("P", 0, 4, 2), ("P", 0, 4, 3), ("wm",), ("first", 0), ("first", 1), ("B", 3), ("P", 1, 3, 0),
    ("P", 1, 3, 1), ("short", 0, 2), ("P", 1, 3, 2), ("P", 1, 3, 3), ("E", 2, 4), ("free", 2),
    ("B", 4), ("free", 3), ("P", 1, 4, 0), ("P", 1, 4, 1), ("free", 4), ("P", 1, 4, 2),
    ("long", 0, 1), ("P", 1, 4, 3), ("first", 2), ("short", 0, 3), ("short", 2, 2), ("first", 3),
    ("short", 3, 2), ("long", 0, 2), ("long", 2, 1), ("first", 4), ("short", 4, 2), ("short", 2, 3),
    ("long", 3, 1), ("short", 3, 3), ("long", 0, 3), ("long", 2, 2), ("long", 4, 1),
    ("short", 4, 3), ("long", 1, 1), ("long", 3, 2), ("short", 1, 2), ("home", 0), ("long", 2, 3),
    ("long", 4, 2), ("long", 1, 2), ("long", 3, 3), ("xs", 0), ("short", 1, 3), ("home", 2),
    ("long", 4, 3), ("long", 1, 3), ("home", 3), ("home", 4), ("zs", 0), ("xs", 2), ("home", 1),
    ("g1",), ("xs", 3), ("zg", 0), ("xs", 4), ("g2",), ("xs", 1), ("zs", 2), ("xg", 0), ("zs", 3),
    ("g3",), ("zs", 4), ("zg", 2), ("zg", 3), ("zs", 1), ("g4",), ("zg", 4), ("xg", 2), ("fin", 0),
    ("xg", 3), ("zg", 1), ("xg", 4), ("fin", 2), ("xg", 1), ("fin", 3), ("fin", 4), ("fin", 1),
)


def dot(a, b):
    return jnp.dot(a, b, preferred_element_type=F32)


def dot_nt(a, b):
    return lax.dot_general(a, b, NT, preferred_element_type=F32)


def kernel(
    routes_hbm, gates_hbm, tok_hbm, grad_hbm, wg_hbm, wu_hbm, wd_hbm,
    mixed, grad_tokens, grad_gates_t,
    routes, gates, rows_in, wg, wu, wd, ag, picked, sums, act, scl, hid, gg, gu, pb, rs_rx, rs_tx,
    ret, ret_tx, pick_t, wm_t, wm, xs_tx, xs_rx, zacc, zs_tx, zs_rx,
    g_tx, g_rx,
    w_sem, in_sem, ag_s, ag_r, rs_s, rs_r, pk_s, pk_r, rt_s, rt_r,
    xs_s, xs_r, zs_s, zs_r, za_s, za_r, xa_s, xa_r, g_s, g_r,
):
    y, t, e = lax.axis_index("dp"), lax.axis_index("tensor"), lax.axis_index("expert")
    n_dp = 8
    zh, core = t // 2, t % 2
    x, zl = e // 4, e % 4
    mirror = x * 4 + 3 - zl
    t1 = 2 * zh + 1 - core
    t2 = 2 * (1 - zh) + core
    t3 = 2 * (1 - zh) + 1 - core
    feats = (t, t1, t2, t3)
    experts = (4 * e + t, 4 * e + t1, 4 * mirror + t2, 4 * mirror + t3)
    peers = (None, (y, t1, e), (y, t2, mirror), (y, t3, mirror))
    up = (lax.rem(y + 1, n_dp), t, e)
    down = (lax.rem(y + n_dp - 1, n_dp), t, e)
    ring = (up, down)
    x_at = [lax.rem(x + rel, 4) for rel in range(4)]
    z_at = [lax.rem(zl + rel, 4) for rel in range(4)]
    x_peers = [(y, t, x_at[rel] * 4 + zl) for rel in range(4)]
    z_peers = [(y, t, x * 4 + z_at[rel]) for rel in range(4)]
    results = (mixed, grad_tokens)

    started = []

    def send(src, dst, s, r, to):
        copy = pltpu.make_async_remote_copy(
            src_ref=src, dst_ref=dst, send_sem=s, recv_sem=r, device_id=to, device_id_type=MESH
        )
        copy.start()
        started.append(copy)
        return copy

    barrier = pltpu.get_barrier_semaphore()
    everyone = list(ring) + list(peers[1:]) + x_peers[1:] + z_peers[1:]
    for peer in everyone:
        pl.semaphore_signal(barrier, inc=1, device_id=peer, device_id_type=MESH)

    row_loads = []
    route_loads = []
    for n, (hbm, vmem) in enumerate(((routes_hbm, routes), (gates_hbm, gates))):
        load = pltpu.make_async_copy(hbm, vmem, in_sem.at[2 + n])
        load.start()
        route_loads.append(load)
    for kind, hbm in enumerate((tok_hbm, grad_hbm)):
        load = pltpu.make_async_copy(hbm, rows_in.at[kind], in_sem.at[kind])
        load.start()
        row_loads.append(load)

    loads = [[], [], []]
    for n, (hbm, vmem) in enumerate(((wg_hbm, wg), (wu_hbm, wu), (wd_hbm, wd))):
        for j in range(4):
            at = pl.multiple_of(feats[j] * 512, 512)
            load = pltpu.make_async_copy(hbm.at[0, :, pl.ds(at, 512)], vmem.at[j], w_sem.at[n, j])
            load.start()
            loads[n].append(load)

    for load in route_loads:
        load.wait()
    ids = routes[...]
    gate_rows = gates[...]
    row8 = lax.broadcasted_iota(jnp.int32, (8, 512), 0)
    masks = []
    chosen = jnp.zeros((8, 512), F32)
    for q in range(4):
        mask = jnp.sum((ids == experts[q]).astype(F32), axis=0, keepdims=True)
        masks.append(mask)
        chosen = chosen + jnp.where(row8 == q, mask, 0.0)
    rows512 = lax.broadcasted_iota(jnp.int32, (512, 512), 0)
    cols512 = lax.broadcasted_iota(jnp.int32, (512, 512), 1)
    before = (rows512 < cols512).astype(F32).astype(BF16)
    rank = dot(chosen.astype(BF16), before).astype(jnp.int32)
    slot = lax.broadcasted_iota(jnp.int32, (CAP, 512), 0)
    for q in range(4):
        hit = (slot == rank[q : q + 1]) & (masks[q] > 0.0)
        gate = jnp.sum(jnp.where(ids == experts[q], gate_rows, 0.0), axis=0, keepdims=True)
        pick_t[48 * q : 48 * q + 48] = jnp.where(hit, 1.0, 0.0).astype(BF16)
        wm_t[48 * q : 48 * q + 48] = jnp.where(hit, gate, 0.0).astype(BF16)

    ag_copy, pk_copy = {}, {}

    def ag_send(kind, way, d, j, src, dst):
        ag_copy[kind, way, d, j] = send(
            ag.at[kind, j, src], ag.at[kind, j, dst],
            ag_s.at[kind, way, d, j], ag_r.at[kind, way, d, j], ring[way],
        )

    def send_own(kind, j):
        ag_send(kind, 0, 0, j, 0, 1)
        ag_send(kind, 1, 0, j, 0, 2)

    for kind in range(2):
        row_loads[kind].wait()
        got = dot(pick_t[...], rows_in[kind]).astype(BF16)
        ag[kind, 0, 0] = got[0:48]
        for q in (2, 3, 1):
            picked[kind, q - 1] = got[48 * q : 48 * q + 48]
        if kind == 0:
            pl.semaphore_wait(barrier, len(everyone))
        for q in (1, 2, 3):
            pk_copy[kind, q] = send(
                picked.at[kind, q - 1], ag.at[kind, q, 0], pk_s.at[kind, q - 1], pk_r.at[kind, q - 1], peers[q]
            )
        send_own(kind, 0)

    here = {(0, 0, 0), (1, 0, 0)}

    def arrived(kind, d, j):
        if (kind, d, j) in here:
            return
        here.add((kind, d, j))
        if d == 0:
            pk_copy[kind, j].wait_recv()
            return
        for way in range(2):
            if d < 4 or j % 2 == way:
                ag_copy[kind, way, d - 1, j].wait_recv()

    def rows_of(kind, j, s0, n):
        return ag[kind, j, s0 : s0 + n].reshape(n * CAP, 512)

    def half_sum(kind, w, j, s0, n):
        both = dot_nt(rows_of(kind, j, s0, n), w[j]) + dot_nt(rows_of(kind, j + 1, s0, n), w[j + 1])
        return both.reshape(n, CAP, 192)

    def span(d):
        return ((0, 1), (1, 2), (3, 2), (5, 2), (ANTI, 1))[d]

    def early(i, d):
        kind, w = ((0, wg), (0, wu), (1, wd))[i]
        while loads[i]:
            loads[i].pop().wait()
        arrived(kind, d, 0)
        arrived(kind, d, 1)
        s0, n = span(d)
        sums[i, s0 : s0 + n] = half_sum(kind, w, 0, s0, n)

    def activate(d):
        arrived(0, d, 2)
        arrived(0, d, 3)
        s0, n = span(d)
        gate_pre = sums[0, s0 : s0 + n] + half_sum(0, wg, 2, s0, n)
        sig = jax.nn.sigmoid(gate_pre)
        act[s0 : s0 + n] = gate_pre * sig
        scl[s0 : s0 + n] = sig * (1.0 + gate_pre * (1.0 - sig))

    def hide(d):
        s0, n = span(d)
        up_pre = sums[1, s0 : s0 + n] + half_sum(0, wu, 2, s0, n)
        hid[s0 : s0 + n] = (act[s0 : s0 + n] * up_pre).astype(BF16)
        scl[s0 : s0 + n] = up_pre * scl[s0 : s0 + n]

    def turn_back(d):
        arrived(1, d, 2)
        arrived(1, d, 3)
        s0, n = span(d)
        grad_hid = sums[2, s0 : s0 + n] + half_sum(1, wd, 2, s0, n)
        gg[s0 : s0 + n] = (grad_hid * scl[s0 : s0 + n]).astype(BF16)
        gu[s0 : s0 + n] = (grad_hid * act[s0 : s0 + n]).astype(BF16)

    def partial(kind, d, j):
        s0, n = span(d)
        if kind == 0:
            part = dot(hid[s0 : s0 + n].reshape(n * CAP, 192), wd[j])
        else:
            part = dot(gg[s0 : s0 + n].reshape(n * CAP, 192), wg[j])
            part = part + dot(gu[s0 : s0 + n].reshape(n * CAP, 192), wu[j])
        part = part.astype(BF16)
        for h in range(2):
            pb[kind, h, s0 : s0 + n, j] = part[:, 256 * h : 256 * h + 256].reshape(n, CAP, 256)

    def gather(kind, d, j):
        arrived(kind, d, j)
        if d == 0:
            send_own(kind, j)
            return
        for way in range(2):
            if d < 3:
                ag_send(kind, way, d, j, 2 * d - 1 + way, 2 * d + 1 + way)
            elif j % 2 == way:
                ag_send(kind, way, d, j, 2 * d - 1 + way, ANTI)

    rs_copy = {}

    def rs_send(u, way, s, p, src):
        kind, h, o, w = UNITS[u]
        rs_copy[u, way, s, p] = send(
            src, rs_rx.at[kind, h, way, s, pl.ds(2 * p, 2), :, pl.ds(o, w)],
            rs_s.at[u, way, s, p], rs_r.at[u, way, s, p], ring[way],
        )

    def first(u):
        kind, h, o, w = UNITS[u]
        for way in range(2):
            rs_send(u, way, 0, way, pb.at[kind, h, ANTI, pl.ds(2 * way, 2), :, pl.ds(o, w)])

    def free(u):
        kind, h, o, w = UNITS[u]
        for way in range(2):
            rs_send(u, way, 1, 1 - way, pb.at[kind, h, 6 - way, pl.ds(2 - 2 * way, 2), :, pl.ds(o, w)])

    def add_on(u, s, turn):
        kind, h, o, w = UNITS[u]
        for way in range(2):
            p = 1 - way if turn == 0 else way
            at, js = 8 - 2 * s - way, slice(2 * p, 2 * p + 2)
            rs_copy[u, way, s - 1, p].wait_recv()
            rs_tx[kind, h, way, s - 1, js, :, o : o + w] = (
                pb[kind, h, at, js, :, o : o + w].astype(F32)
                + rs_rx[kind, h, way, s - 1, js, :, o : o + w].astype(F32)
            ).astype(BF16)
        for way in range(2):
            p = 1 - way if turn == 0 else way
            src = rs_tx.at[kind, h, way, s - 1, pl.ds(2 * p, 2), :, pl.ds(o, w)]
            rs_send(u, way, s, p, src)

    def long(u, s):
        add_on(u, s, 1)

    def short(u, s):
        add_on(u, s, 0)

    rt_copy, g_copy, e_copy = {}, {}, {}
    products = []

    def home(u):
        kind, h, o, w = UNITS[u]
        lanes = slice(o, o + w)
        for p in (1, 0):
            for way in range(2):
                rs_copy[u, way, 3, p].wait_recv()
            for j in (2 * p + 1, 2 * p):
                total = (
                    pb[kind, h, 0, j, :, lanes].astype(F32)
                    + rs_rx[kind, h, 0, 3, j, :, lanes].astype(F32)
                    + rs_rx[kind, h, 1, 3, j, :, lanes].astype(F32)
                ).astype(BF16)
                if j == 0:
                    ret[kind, h, 0:48, lanes] = total
                else:
                    ret_tx[kind, h, j - 1, :, lanes] = total
                if kind == 0:
                    theirs = ag[1, j, 0, :, 256 * h : 256 * h + 256].astype(F32)
                    products.append(jnp.sum(total.astype(F32) * theirs, axis=1, keepdims=True))
            for j in (2 * p + 1, 2 * p):
                if j:
                    rt_copy[u, j] = send(
                        ret_tx.at[kind, h, j - 1, :, pl.ds(o, w)],
                        ret.at[kind, h, pl.ds(48 * j, 48), pl.ds(o, w)],
                        rt_s.at[u, j - 1], rt_r.at[u, j - 1], peers[j],
                    )

    def gates_send(stage, block, to):
        g_tx[stage] = block
        for i in range(3):
            g_copy[stage, i] = send(
                g_tx.at[stage], g_rx.at[stage, i], g_s.at[stage, i], g_r.at[stage, i], to[i + 1]
            )

    def gates_sum(stage):
        block = g_tx[stage]
        for i in range(3):
            g_copy[stage, i].wait_recv()
            block = block + g_rx[stage, i]
        return block

    def gates_first():
        total = products[0]
        for term in products[1:]:
            total = total + term
        own = jnp.sum(pick_t[0:48].astype(F32) * total, axis=0, keepdims=True)
        gates_send(0, jnp.where(routes[...] == experts[0], own, 0.0), peers)

    def gates_second():
        gates_send(1, gates_sum(0), x_peers)

    def gates_third():
        gates_send(2, gates_sum(1), z_peers)

    def gates_last():
        grad_gates_t[...] = gates_sum(2)

    def x_scatter(u):
        kind, h, o, w = UNITS[u]
        for j in (1, 2, 3):
            rt_copy[u, j].wait_recv()
        slots = ret[kind, h, :, o : o + w]
        for rel in (2, 1, 3):
            rows = pl.ds(pl.multiple_of(x_at[rel] * 128, 128), 128)
            xs_tx[kind, h, rel - 1, :, o : o + w] = dot(wm[rows], slots).astype(BF16)
        for rel in (2, 1, 3):
            e_copy["xs", u, rel] = send(
                xs_tx.at[kind, h, rel - 1, :, pl.ds(o, w)], xs_rx.at[kind, h, rel - 1, :, pl.ds(o, w)],
                xs_s.at[u, rel - 1], xs_r.at[u, rel - 1], x_peers[rel],
            )
        zacc[kind, h, :, o : o + w] = dot(wm[pl.ds(pl.multiple_of(x * 128, 128), 128)], slots)

    def z_scatter(u):
        kind, h, o, w = UNITS[u]
        for rel in (1, 3, 2):
            e_copy["xs", u, rel].wait_recv()
        total = zacc[kind, h, :, o : o + w]
        for rel in range(1, 4):
            total = total + xs_rx[kind, h, rel - 1, :, o : o + w].astype(F32)
        zacc[kind, h, :, o : o + w] = total
        zs_tx[kind, h, :, o : o + w] = total.astype(BF16)
        for rel in (2, 1, 3):
            rows = pl.ds(pl.multiple_of(z_at[rel] * 32, 32), 32)
            e_copy["zs", u, rel] = send(
                zs_tx.at[kind, h, rows, pl.ds(o, w)], zs_rx.at[kind, h, rel - 1, :, pl.ds(o, w)],
                zs_s.at[u, rel - 1], zs_r.at[u, rel - 1], z_peers[rel],
            )

    def z_gather(u):
        kind, h, o, w = UNITS[u]
        total = zacc[kind, h, pl.ds(pl.multiple_of(zl * 32, 32), 32), o : o + w]
        for rel in (1, 3, 2):
            e_copy["zs", u, rel].wait_recv()
        for rel in range(1, 4):
            total = total + zs_rx[kind, h, rel - 1, :, o : o + w].astype(F32)
        rows = pl.ds(pl.multiple_of(x * 128 + zl * 32, 32), 32)
        out = results[kind]
        out[rows, 256 * h + o : 256 * h + o + w] = total.astype(BF16)
        place = out.at[rows, pl.ds(256 * h + o, w)]
        for rel in (2, 1, 3):
            e_copy["za", u, rel] = send(place, place, za_s.at[u, rel - 1], za_r.at[u, rel - 1], z_peers[rel])

    def x_gather(u):
        kind, h, o, w = UNITS[u]
        for rel in (1, 3, 2):
            e_copy["za", u, rel].wait_recv()
        rows = pl.ds(pl.multiple_of(x * 128, 128), 128)
        place = results[kind].at[rows, pl.ds(256 * h + o, w)]
        for rel in (2, 1, 3):
            e_copy["xa", u, rel] = send(place, place, xa_s.at[u, rel - 1], xa_r.at[u, rel - 1], x_peers[rel])

    def finish(u):
        for rel in (1, 3, 2):
            e_copy["xa", u, rel].wait_recv()

    def weigh():
        wm[...] = dot_nt((rows512 == cols512).astype(F32).astype(BF16), wm_t[...]).astype(BF16)

    steps = {
        "ag": gather, "E": early, "F": activate, "G": hide, "B": turn_back, "P": partial,
        "first": first, "free": free, "long": long, "short": short, "home": home,
        "xs": x_scatter, "zs": z_scatter, "zg": z_gather, "xg": x_gather, "fin": finish,
        "g1": gates_first, "g2": gates_second, "g3": gates_third, "g4": gates_last, "wm": weigh,
    }
    for name, *at in PLAN:
        steps[name](*at)
    for copy in started:
        copy.wait_send()


def body(tokens, grad_out, routes, gates, gate_weight, up_weight, down_weight):
    vmem = pl.BlockSpec(memory_space=pltpu.VMEM)
    hbm = pl.BlockSpec(memory_space=pltpu.HBM)
    dma = pltpu.SemaphoreType.DMA
    operands = (routes.T, gates.T, tokens, grad_out, gate_weight, up_weight, down_weight)
    mixed, grad_tokens, grad_gates_t = pl.pallas_call(
        kernel,
        out_shape=(
            jax.ShapeDtypeStruct((512, 512), BF16),
            jax.ShapeDtypeStruct((512, 512), BF16),
            jax.ShapeDtypeStruct((8, 512), F32),
        ),
        in_specs=[hbm] * 7,
        out_specs=(vmem, vmem, vmem),
        scratch_shapes=[
            pltpu.VMEM((8, 512), jnp.int32),
            pltpu.VMEM((8, 512), F32),
            pltpu.VMEM((2, 512, 512), BF16),
            pltpu.VMEM((4, 192, 512), BF16),
            pltpu.VMEM((4, 192, 512), BF16),
            pltpu.VMEM((4, 192, 512), BF16),
            pltpu.VMEM((2, 4, 8, CAP, 512), BF16),
            pltpu.VMEM((2, 3, CAP, 512), BF16),
            pltpu.VMEM((3, 8, CAP, 192), F32),
            pltpu.VMEM((8, CAP, 192), F32),
            pltpu.VMEM((8, CAP, 192), F32),
            pltpu.VMEM((8, CAP, 192), BF16),
            pltpu.VMEM((8, CAP, 192), BF16),
            pltpu.VMEM((8, CAP, 192), BF16),
            pltpu.VMEM((2, 2, 8, 4, CAP, 256), BF16),
            pltpu.VMEM((2, 2, 2, 4, 4, CAP, 256), BF16),
            pltpu.VMEM((2, 2, 2, 3, 4, CAP, 256), BF16),
            pltpu.VMEM((2, 2, 192, 256), BF16),
            pltpu.VMEM((2, 2, 3, CAP, 256), BF16),
            pltpu.VMEM((192, 512), BF16),
            pltpu.VMEM((192, 512), BF16),
            pltpu.VMEM((512, 192), BF16),
            pltpu.VMEM((2, 2, 3, 128, 256), BF16),
            pltpu.VMEM((2, 2, 3, 128, 256), BF16),
            pltpu.VMEM((2, 2, 128, 256), F32),
            pltpu.VMEM((2, 2, 128, 256), BF16),
            pltpu.VMEM((2, 2, 3, 32, 256), BF16),
            pltpu.VMEM((3, 8, 512), F32),
            pltpu.VMEM((3, 3, 8, 512), F32),
            dma((3, 4)),
            dma((4,)),
            dma((2, 2, 4, 4)),
            dma((2, 2, 4, 4)),
            dma((5, 2, 4, 2)),
            dma((5, 2, 4, 2)),
            dma((2, 3)),
            dma((2, 3)),
        ]
        + [dma((5, 3))] * 10
        + [dma((3, 3))] * 2,
        compiler_params=pltpu.CompilerParams(
            collective_id=0, has_side_effects=True, vmem_limit_bytes=40 * 1024 * 1024
        ),
    )(*[pltpu.with_memory_space_constraint(a, pltpu.HBM) for a in operands])
    return mixed, grad_tokens, grad_gates_t.T


def solution(mesh):
    return jax.shard_map(
        body,
        mesh=mesh,
        in_specs=(
            P("dp", "tensor"),
            P("dp", "tensor"),
            P("dp", None),
            P("dp", None),
            P(("expert", "tensor"), "dp", None),
            P(("expert", "tensor"), "dp", None),
            P(("expert", "tensor"), "dp", None),
        ),
        out_specs=(P("dp", "tensor"), P("dp", "tensor"), P("dp", None)),
        check_vma=False,
    )
```

```python
import jax
import jax.numpy as jnp
from jax import lax
from jax.experimental import pallas as pl
from jax.experimental.pallas import tpu as pltpu
from jax.sharding import PartitionSpec as P

CAP = 48
MESH = pl.DeviceIdType.MESH
F32 = jnp.float32
BF16 = jnp.bfloat16
NT = (((1,), (1,)), ((), ()))
ANTI = 7
UNITS = ((0, 0, 0, 256), (0, 1, 0, 256), (1, 0, 0, 256), (1, 1, 0, 128), (1, 1, 128, 128))
PLAN = (
    ("wm",), ("ag", 0, 0, 1), ("E", 0, 0), ("E", 1, 0), ("ag", 0, 1, 0), ("ag", 1, 0, 1), ("E", 2, 0),
    ("ag", 1, 1, 0), ("ag", 0, 1, 1), ("E", 0, 1), ("E", 1, 1), ("ag", 0, 2, 0), ("ag", 0, 0, 2),
    ("F", 0), ("ag", 0, 0, 3), ("G", 0), ("P", 0, 0, 0), ("P", 0, 0, 1), ("P", 0, 0, 2),
    ("ag", 1, 1, 1), ("P", 0, 0, 3), ("E", 2, 1), ("E", 0, 2), ("ag", 0, 2, 1), ("E", 1, 2),
    ("ag", 0, 3, 0), ("B", 0), ("P", 1, 0, 0), ("ag", 1, 0, 2), ("P", 1, 0, 1), ("P", 1, 0, 2),
    ("P", 1, 0, 3), ("ag", 0, 1, 2), ("F", 1), ("G", 1), ("P", 0, 1, 0), ("ag", 0, 1, 3),
    ("P", 0, 1, 1), ("P", 0, 1, 2), ("P", 0, 1, 3), ("E", 2, 2), ("ag", 1, 0, 3), ("E", 0, 3),
    ("E", 1, 3), ("ag", 0, 3, 1), ("ag", 1, 2, 0), ("ag", 1, 1, 2), ("ag", 0, 2, 2), ("F", 2),
    ("G", 2), ("P", 0, 2, 0), ("ag", 0, 2, 3), ("P", 0, 2, 1), ("P", 0, 2, 2), ("P", 0, 2, 3),
    ("E", 0, 4), ("ag", 1, 1, 3), ("E", 1, 4), ("B", 1), ("P", 1, 1, 0), ("ag", 1, 2, 1),
    ("P", 1, 1, 1), ("P", 1, 1, 2), ("P", 1, 1, 3), ("ag", 1, 2, 2), ("ag", 0, 3, 2),
    ("ag", 1, 3, 0), ("F", 3), ("ag", 0, 3, 3), ("G", 3), ("P", 0, 3, 0), ("P", 0, 3, 1),
    ("ag", 1, 2, 3), ("P", 0, 3, 2), ("P", 0, 3, 3), ("free", 0), ("B", 2), ("E", 2, 3),
    ("P", 1, 2, 0), ("P", 1, 2, 1), ("free", 1), ("P", 1, 2, 2), ("P", 1, 2, 3), ("ag", 1, 3, 1),
    ("ag", 1, 3, 2), ("F", 4), ("G", 4), ("P", 0, 4, 0), ("P", 0, 4, 1), ("ag", 1, 3, 3),
    ("P", 0, 4, 2), ("P", 0, 4, 3), ("first", 0), ("first", 1), ("B", 3), ("P", 1, 3, 0),
    ("P", 1, 3, 1), ("short", 0, 2), ("P", 1, 3, 2), ("P", 1, 3, 3), ("E", 2, 4), ("free", 2),
    ("B", 4), ("free", 3), ("P", 1, 4, 0), ("P", 1, 4, 1), ("free", 4), ("P", 1, 4, 2),
    ("long", 0, 1), ("P", 1, 4, 3), ("first", 2), ("short", 0, 3), ("short", 2, 2), ("first", 3),
    ("short", 3, 2), ("long", 0, 2), ("long", 2, 1), ("first", 4), ("short", 4, 2), ("short", 2, 3),
    ("long", 3, 1), ("short", 3, 3), ("long", 0, 3), ("long", 2, 2), ("long", 4, 1),
    ("short", 4, 3), ("long", 1, 1), ("long", 3, 2), ("short", 1, 2), ("home", 0), ("long", 2, 3),
    ("long", 4, 2), ("long", 1, 2), ("long", 3, 3), ("xs", 0), ("short", 1, 3), ("home", 2),
    ("long", 4, 3), ("long", 1, 3), ("home", 3), ("home", 4), ("zs", 0), ("xs", 2), ("home", 1),
    ("g1",), ("xs", 3), ("zg", 0), ("xs", 4), ("g2",), ("xs", 1), ("zs", 2), ("xg", 0), ("zs", 3),
    ("g3",), ("zs", 4), ("zg", 2), ("zg", 3), ("zs", 1), ("g4",), ("zg", 4), ("xg", 2), ("fin", 0),
    ("xg", 3), ("zg", 1), ("xg", 4), ("fin", 2), ("xg", 1), ("fin", 3), ("fin", 4), ("fin", 1),
)


def dot(a, b):
    return jnp.dot(a, b, preferred_element_type=F32)


def dot_nt(a, b):
    return lax.dot_general(a, b, NT, preferred_element_type=F32)


def kernel(
    routes_hbm, gates_hbm, tok_hbm, grad_hbm, wg_hbm, wu_hbm, wd_hbm,
    mixed, grad_tokens, grad_gates_t,
    routes, gates, rows_in, wg, wu, wd, ag, picked, sums, act, scl, hid, gg, gu, pb, rs_rx, rs_tx,
    ret, ret_tx, pick_t, wm_t, wm, xs_tx, xs_rx, zacc, zs_tx, zs_rx,
    g_tx, g_rx,
    w_sem, in_sem, ag_s, ag_r, rs_s, rs_r, pk_s, pk_r, rt_s, rt_r,
    xs_s, xs_r, zs_s, zs_r, za_s, za_r, xa_s, xa_r, g_s, g_r,
):
    y, t, e = lax.axis_index("dp"), lax.axis_index("tensor"), lax.axis_index("expert")
    n_dp = 8
    zh, core = t // 2, t % 2
    x, zl = e // 4, e % 4
    mirror = x * 4 + 3 - zl
    t1 = 2 * zh + 1 - core
    t2 = 2 * (1 - zh) + core
    t3 = 2 * (1 - zh) + 1 - core
    feats = (t, t1, t2, t3)
    experts = (4 * e + t, 4 * e + t1, 4 * mirror + t2, 4 * mirror + t3)
    peers = (None, (y, t1, e), (y, t2, mirror), (y, t3, mirror))
    up = (lax.rem(y + 1, n_dp), t, e)
    down = (lax.rem(y + n_dp - 1, n_dp), t, e)
    ring = (up, down)
    x_at = [lax.rem(x + rel, 4) for rel in range(4)]
    z_at = [lax.rem(zl + rel, 4) for rel in range(4)]
    x_peers = [(y, t, x_at[rel] * 4 + zl) for rel in range(4)]
    z_peers = [(y, t, x * 4 + z_at[rel]) for rel in range(4)]
    results = (mixed, grad_tokens)

    started = []

    def send(src, dst, s, r, to):
        copy = pltpu.make_async_remote_copy(
            src_ref=src, dst_ref=dst, send_sem=s, recv_sem=r, device_id=to, device_id_type=MESH
        )
        copy.start()
        started.append(copy)
        return copy

    row_loads = []
    route_loads = []
    for n, (hbm, vmem) in enumerate(((routes_hbm, routes), (gates_hbm, gates))):
        load = pltpu.make_async_copy(hbm, vmem, in_sem.at[2 + n])
        load.start()
        route_loads.append(load)

    barrier = pltpu.get_barrier_semaphore()
    everyone = list(ring) + list(peers[1:]) + x_peers[1:] + z_peers[1:]
    for peer in everyone:
        pl.semaphore_signal(barrier, inc=1, device_id=peer, device_id_type=MESH)

    for kind, hbm in enumerate((tok_hbm, grad_hbm)):
        load = pltpu.make_async_copy(hbm, rows_in.at[kind], in_sem.at[kind])
        load.start()
        row_loads.append(load)

    loads = [[], [], []]
    for n, (hbm, vmem) in enumerate(((wg_hbm, wg), (wu_hbm, wu), (wd_hbm, wd))):
        for j in range(4):
            at = pl.multiple_of(feats[j] * 512, 512)
            load = pltpu.make_async_copy(hbm.at[0, :, pl.ds(at, 512)], vmem.at[j], w_sem.at[n, j])
            load.start()
            loads[n].append(load)

    rows512 = lax.broadcasted_iota(jnp.int32, (512, 512), 0)
    cols512 = lax.broadcasted_iota(jnp.int32, (512, 512), 1)
    before = (rows512 < cols512).astype(F32).astype(BF16)
    for load in route_loads:
        load.wait()
    ids = routes[...]
    gate_rows = gates[...]
    row8 = lax.broadcasted_iota(jnp.int32, (8, 512), 0)
    masks = []
    chosen = jnp.zeros((8, 512), F32)
    for q in range(4):
        mask = jnp.sum((ids == experts[q]).astype(F32), axis=0, keepdims=True)
        masks.append(mask)
        chosen = chosen + jnp.where(row8 == q, mask, 0.0)
    rank = dot(chosen.astype(BF16), before).astype(jnp.int32)
    slot = lax.broadcasted_iota(jnp.int32, (CAP, 512), 0)
    for q in range(4):
        hit = (slot == rank[q : q + 1]) & (masks[q] > 0.0)
        gate = jnp.sum(jnp.where(ids == experts[q], gate_rows, 0.0), axis=0, keepdims=True)
        pick_t[48 * q : 48 * q + 48] = jnp.where(hit, 1.0, 0.0).astype(BF16)
        wm_t[48 * q : 48 * q + 48] = jnp.where(hit, gate, 0.0).astype(BF16)

    ag_copy, pk_copy = {}, {}

    def ag_send(kind, way, d, j, src, dst):
        ag_copy[kind, way, d, j] = send(
            ag.at[kind, j, src], ag.at[kind, j, dst],
            ag_s.at[kind, way, d, j], ag_r.at[kind, way, d, j], ring[way],
        )

    def send_own(kind, j):
        ag_send(kind, 0, 0, j, 0, 1)
        ag_send(kind, 1, 0, j, 0, 2)

    for kind in range(2):
        row_loads[kind].wait()
        got = dot(pick_t[...], rows_in[kind]).astype(BF16)
        ag[kind, 0, 0] = got[0:48]
        for q in (2, 3, 1):
            picked[kind, q - 1] = got[48 * q : 48 * q + 48]
        if kind == 0:
            pl.semaphore_wait(barrier, len(everyone))
        for q in (1, 2, 3):
            pk_copy[kind, q] = send(
                picked.at[kind, q - 1], ag.at[kind, q, 0], pk_s.at[kind, q - 1], pk_r.at[kind, q - 1], peers[q]
            )
        send_own(kind, 0)

    here = {(0, 0, 0), (1, 0, 0)}

    def arrived(kind, d, j):
        if (kind, d, j) in here:
            return
        here.add((kind, d, j))
        if d == 0:
            pk_copy[kind, j].wait_recv()
            return
        for way in range(2):
            if d < 4 or j % 2 == way:
                ag_copy[kind, way, d - 1, j].wait_recv()

    def rows_of(kind, j, s0, n):
        return ag[kind, j, s0 : s0 + n].reshape(n * CAP, 512)

    def half_sum(kind, w, j, s0, n):
        both = dot_nt(rows_of(kind, j, s0, n), w[j]) + dot_nt(rows_of(kind, j + 1, s0, n), w[j + 1])
        return both.reshape(n, CAP, 192)

    def span(d):
        return ((0, 1), (1, 2), (3, 2), (5, 2), (ANTI, 1))[d]

    def early(i, d):
        kind, w = ((0, wg), (0, wu), (1, wd))[i]
        while loads[i]:
            loads[i].pop().wait()
        arrived(kind, d, 0)
        arrived(kind, d, 1)
        s0, n = span(d)
        sums[i, s0 : s0 + n] = half_sum(kind, w, 0, s0, n)

    def activate(d):
        arrived(0, d, 2)
        arrived(0, d, 3)
        s0, n = span(d)
        gate_pre = sums[0, s0 : s0 + n] + half_sum(0, wg, 2, s0, n)
        sig = jax.nn.sigmoid(gate_pre)
        act[s0 : s0 + n] = gate_pre * sig
        scl[s0 : s0 + n] = sig * (1.0 + gate_pre * (1.0 - sig))

    def hide(d):
        s0, n = span(d)
        up_pre = sums[1, s0 : s0 + n] + half_sum(0, wu, 2, s0, n)
        hid[s0 : s0 + n] = (act[s0 : s0 + n] * up_pre).astype(BF16)
        scl[s0 : s0 + n] = up_pre * scl[s0 : s0 + n]

    def turn_back(d):
        arrived(1, d, 2)
        arrived(1, d, 3)
        s0, n = span(d)
        grad_hid = sums[2, s0 : s0 + n] + half_sum(1, wd, 2, s0, n)
        gg[s0 : s0 + n] = (grad_hid * scl[s0 : s0 + n]).astype(BF16)
        gu[s0 : s0 + n] = (grad_hid * act[s0 : s0 + n]).astype(BF16)

    def partial(kind, d, j):
        s0, n = span(d)
        if kind == 0:
            part = dot(hid[s0 : s0 + n].reshape(n * CAP, 192), wd[j])
        else:
            part = dot(gg[s0 : s0 + n].reshape(n * CAP, 192), wg[j])
            part = part + dot(gu[s0 : s0 + n].reshape(n * CAP, 192), wu[j])
        part = part.astype(BF16)
        for h in range(2):
            pb[kind, h, s0 : s0 + n, j] = part[:, 256 * h : 256 * h + 256].reshape(n, CAP, 256)

    def gather(kind, d, j):
        arrived(kind, d, j)
        if d == 0:
            send_own(kind, j)
            return
        for way in range(2):
            if d < 3:
                ag_send(kind, way, d, j, 2 * d - 1 + way, 2 * d + 1 + way)
            elif j % 2 == way:
                ag_send(kind, way, d, j, 2 * d - 1 + way, ANTI)

    rs_copy = {}

    def rs_send(u, way, s, p, src):
        kind, h, o, w = UNITS[u]
        rs_copy[u, way, s, p] = send(
            src, rs_rx.at[kind, h, way, s, pl.ds(2 * p, 2), :, pl.ds(o, w)],
            rs_s.at[u, way, s, p], rs_r.at[u, way, s, p], ring[way],
        )

    def first(u):
        kind, h, o, w = UNITS[u]
        for way in range(2):
            rs_send(u, way, 0, way, pb.at[kind, h, ANTI, pl.ds(2 * way, 2), :, pl.ds(o, w)])

    def free(u):
        kind, h, o, w = UNITS[u]
        for way in range(2):
            rs_send(u, way, 1, 1 - way, pb.at[kind, h, 6 - way, pl.ds(2 - 2 * way, 2), :, pl.ds(o, w)])

    def add_on(u, s, turn):
        kind, h, o, w = UNITS[u]
        for way in range(2):
            p = 1 - way if turn == 0 else way
            at, js = 8 - 2 * s - way, slice(2 * p, 2 * p + 2)
            rs_copy[u, way, s - 1, p].wait_recv()
            rs_tx[kind, h, way, s - 1, js, :, o : o + w] = (
                pb[kind, h, at, js, :, o : o + w].astype(F32)
                + rs_rx[kind, h, way, s - 1, js, :, o : o + w].astype(F32)
            ).astype(BF16)
        for way in range(2):
            p = 1 - way if turn == 0 else way
            src = rs_tx.at[kind, h, way, s - 1, pl.ds(2 * p, 2), :, pl.ds(o, w)]
            rs_send(u, way, s, p, src)

    def long(u, s):
        add_on(u, s, 1)

    def short(u, s):
        add_on(u, s, 0)

    rt_copy, g_copy, e_copy = {}, {}, {}
    products = []

    def home(u):
        kind, h, o, w = UNITS[u]
        lanes = slice(o, o + w)
        for p in (1, 0):
            for way in range(2):
                rs_copy[u, way, 3, p].wait_recv()
            for j in (2 * p + 1, 2 * p):
                total = (
                    pb[kind, h, 0, j, :, lanes].astype(F32)
                    + rs_rx[kind, h, 0, 3, j, :, lanes].astype(F32)
                    + rs_rx[kind, h, 1, 3, j, :, lanes].astype(F32)
                ).astype(BF16)
                if j == 0:
                    ret[kind, h, 0:48, lanes] = total
                else:
                    ret_tx[kind, h, j - 1, :, lanes] = total
                if kind == 0:
                    theirs = ag[1, j, 0, :, 256 * h : 256 * h + 256].astype(F32)
                    products.append(jnp.sum(total.astype(F32) * theirs, axis=1, keepdims=True))
            for j in (2 * p + 1, 2 * p):
                if j:
                    rt_copy[u, j] = send(
                        ret_tx.at[kind, h, j - 1, :, pl.ds(o, w)],
                        ret.at[kind, h, pl.ds(48 * j, 48), pl.ds(o, w)],
                        rt_s.at[u, j - 1], rt_r.at[u, j - 1], peers[j],
                    )

    def gates_send(stage, block, to):
        g_tx[stage] = block
        for i in range(3):
            g_copy[stage, i] = send(
                g_tx.at[stage], g_rx.at[stage, i], g_s.at[stage, i], g_r.at[stage, i], to[i + 1]
            )

    def gates_sum(stage):
        block = g_tx[stage]
        for i in range(3):
            g_copy[stage, i].wait_recv()
            block = block + g_rx[stage, i]
        return block

    def gates_first():
        total = products[0]
        for term in products[1:]:
            total = total + term
        own = jnp.sum(pick_t[0:48].astype(F32) * total, axis=0, keepdims=True)
        gates_send(0, jnp.where(routes[...] == experts[0], own, 0.0), peers)

    def gates_second():
        gates_send(1, gates_sum(0), x_peers)

    def gates_third():
        gates_send(2, gates_sum(1), z_peers)

    def gates_last():
        grad_gates_t[...] = gates_sum(2)

    def x_scatter(u):
        kind, h, o, w = UNITS[u]
        for j in (1, 2, 3):
            rt_copy[u, j].wait_recv()
        slots = ret[kind, h, :, o : o + w]
        for rel in (2, 1, 3):
            rows = pl.ds(pl.multiple_of(x_at[rel] * 128, 128), 128)
            xs_tx[kind, h, rel - 1, :, o : o + w] = dot(wm[rows], slots).astype(BF16)
        for rel in (2, 1, 3):
            e_copy["xs", u, rel] = send(
                xs_tx.at[kind, h, rel - 1, :, pl.ds(o, w)], xs_rx.at[kind, h, rel - 1, :, pl.ds(o, w)],
                xs_s.at[u, rel - 1], xs_r.at[u, rel - 1], x_peers[rel],
            )
        zacc[kind, h, :, o : o + w] = dot(wm[pl.ds(pl.multiple_of(x * 128, 128), 128)], slots)

    def z_scatter(u):
        kind, h, o, w = UNITS[u]
        for rel in (1, 3, 2):
            e_copy["xs", u, rel].wait_recv()
        total = zacc[kind, h, :, o : o + w]
        for rel in range(1, 4):
            total = total + xs_rx[kind, h, rel - 1, :, o : o + w].astype(F32)
        zacc[kind, h, :, o : o + w] = total
        zs_tx[kind, h, :, o : o + w] = total.astype(BF16)
        for rel in (2, 1, 3):
            rows = pl.ds(pl.multiple_of(z_at[rel] * 32, 32), 32)
            e_copy["zs", u, rel] = send(
                zs_tx.at[kind, h, rows, pl.ds(o, w)], zs_rx.at[kind, h, rel - 1, :, pl.ds(o, w)],
                zs_s.at[u, rel - 1], zs_r.at[u, rel - 1], z_peers[rel],
            )

    def z_gather(u):
        kind, h, o, w = UNITS[u]
        total = zacc[kind, h, pl.ds(pl.multiple_of(zl * 32, 32), 32), o : o + w]
        for rel in (1, 3, 2):
            e_copy["zs", u, rel].wait_recv()
        for rel in range(1, 4):
            total = total + zs_rx[kind, h, rel - 1, :, o : o + w].astype(F32)
        rows = pl.ds(pl.multiple_of(x * 128 + zl * 32, 32), 32)
        out = results[kind]
        out[rows, 256 * h + o : 256 * h + o + w] = total.astype(BF16)
        place = out.at[rows, pl.ds(256 * h + o, w)]
        for rel in (2, 1, 3):
            e_copy["za", u, rel] = send(place, place, za_s.at[u, rel - 1], za_r.at[u, rel - 1], z_peers[rel])

    def x_gather(u):
        kind, h, o, w = UNITS[u]
        for rel in (1, 3, 2):
            e_copy["za", u, rel].wait_recv()
        rows = pl.ds(pl.multiple_of(x * 128, 128), 128)
        place = results[kind].at[rows, pl.ds(256 * h + o, w)]
        for rel in (2, 1, 3):
            e_copy["xa", u, rel] = send(place, place, xa_s.at[u, rel - 1], xa_r.at[u, rel - 1], x_peers[rel])

    def finish(u):
        for rel in (1, 3, 2):
            e_copy["xa", u, rel].wait_recv()

    def weigh():
        wm[...] = dot_nt((rows512 == cols512).astype(F32).astype(BF16), wm_t[...]).astype(BF16)

    steps = {
        "ag": gather, "E": early, "F": activate, "G": hide, "B": turn_back, "P": partial,
        "first": first, "free": free, "long": long, "short": short, "home": home,
        "xs": x_scatter, "zs": z_scatter, "zg": z_gather, "xg": x_gather, "fin": finish,
        "g1": gates_first, "g2": gates_second, "g3": gates_third, "g4": gates_last, "wm": weigh,
    }
    for name, *at in PLAN:
        steps[name](*at)
    for copy in started:
        copy.wait_send()


def body(tokens, grad_out, routes, gates, gate_weight, up_weight, down_weight):
    vmem = pl.BlockSpec(memory_space=pltpu.VMEM)
    hbm = pl.BlockSpec(memory_space=pltpu.HBM)
    dma = pltpu.SemaphoreType.DMA
    operands = (routes.T, gates.T, tokens, grad_out, gate_weight, up_weight, down_weight)
    mixed, grad_tokens, grad_gates_t = pl.pallas_call(
        kernel,
        out_shape=(
            jax.ShapeDtypeStruct((512, 512), BF16),
            jax.ShapeDtypeStruct((512, 512), BF16),
            jax.ShapeDtypeStruct((8, 512), F32),
        ),
        in_specs=[hbm] * 7,
        out_specs=(vmem, vmem, vmem),
        scratch_shapes=[
            pltpu.VMEM((8, 512), jnp.int32),
            pltpu.VMEM((8, 512), F32),
            pltpu.VMEM((2, 512, 512), BF16),
            pltpu.VMEM((4, 192, 512), BF16),
            pltpu.VMEM((4, 192, 512), BF16),
            pltpu.VMEM((4, 192, 512), BF16),
            pltpu.VMEM((2, 4, 8, CAP, 512), BF16),
            pltpu.VMEM((2, 3, CAP, 512), BF16),
            pltpu.VMEM((3, 8, CAP, 192), F32),
            pltpu.VMEM((8, CAP, 192), F32),
            pltpu.VMEM((8, CAP, 192), F32),
            pltpu.VMEM((8, CAP, 192), BF16),
            pltpu.VMEM((8, CAP, 192), BF16),
            pltpu.VMEM((8, CAP, 192), BF16),
            pltpu.VMEM((2, 2, 8, 4, CAP, 256), BF16),
            pltpu.VMEM((2, 2, 2, 4, 4, CAP, 256), BF16),
            pltpu.VMEM((2, 2, 2, 3, 4, CAP, 256), BF16),
            pltpu.VMEM((2, 2, 192, 256), BF16),
            pltpu.VMEM((2, 2, 3, CAP, 256), BF16),
            pltpu.VMEM((192, 512), BF16),
            pltpu.VMEM((192, 512), BF16),
            pltpu.VMEM((512, 192), BF16),
            pltpu.VMEM((2, 2, 3, 128, 256), BF16),
            pltpu.VMEM((2, 2, 3, 128, 256), BF16),
            pltpu.VMEM((2, 2, 128, 256), F32),
            pltpu.VMEM((2, 2, 128, 256), BF16),
            pltpu.VMEM((2, 2, 3, 32, 256), BF16),
            pltpu.VMEM((3, 8, 512), F32),
            pltpu.VMEM((3, 3, 8, 512), F32),
            dma((3, 4)),
            dma((4,)),
            dma((2, 2, 4, 4)),
            dma((2, 2, 4, 4)),
            dma((5, 2, 4, 2)),
            dma((5, 2, 4, 2)),
            dma((2, 3)),
            dma((2, 3)),
        ]
        + [dma((5, 3))] * 10
        + [dma((3, 3))] * 2,
        compiler_params=pltpu.CompilerParams(
            collective_id=0, has_side_effects=True, vmem_limit_bytes=40 * 1024 * 1024
        ),
    )(*[pltpu.with_memory_space_constraint(a, pltpu.HBM) for a in operands])
    return mixed, grad_tokens, grad_gates_t.T


def solution(mesh):
    return jax.shard_map(
        body,
        mesh=mesh,
        in_specs=(
            P("dp", "tensor"),
            P("dp", "tensor"),
            P("dp", None),
            P("dp", None),
            P(("expert", "tensor"), "dp", None),
            P(("expert", "tensor"), "dp", None),
            P(("expert", "tensor"), "dp", None),
        ),
        out_specs=(P("dp", "tensor"), P("dp", "tensor"), P("dp", None)),
        check_vma=False,
    )
```
